128 devices in a mesh: row: 16 (over x, y), col: 8 (over z, core).
Axes of the slice: x: 4, y: 4, z: 4, core: 2. Of those that a mesh axis runs over, the one named last changes fastest.
Arguments:
- sources: bfloat16 [16, 32768], P(None, ('row', 'col')), may hold values from -6 to 6
- dipole_tiles: bfloat16 [4096, 256, 256], P(('row', 'col')), may hold values from -0.1875 to 0.1875
- dipole_rows: int32 [4096], P(('row', 'col')), may hold values from 0 to 7
- dipole_columns: int32 [4096], P(('row', 'col')), may hold values from 0 to 15
- dipole_count: int32 [128], P(('row', 'col')), may hold values from 1 to 32, as said below
- energies: float32 [32768], P(('row', 'col')), may hold values from -3 to 3
- h_tiles: bfloat16 [4096, 256, 256], P(('row', 'col')), may hold values from -0.0625 to 0.0625
- tile_rows: int32 [4096], P(('row', 'col')), may hold values from 0 to 7, as said below
- tile_columns: int32 [4096], P(('row', 'col')), may hold values from 0 to 15
- tile_count: int32 [128], P(('row', 'col')), may hold values from 1 to 32, as said below
Outputs:
- solution: float32 [64, 32768], P(None, ('row', 'col'))
- residual: float32 [64, 32768], P(None, ('row', 'col'))
- checksum: float32 [3, 64], replicated
The draws below stay inside these ranges and needn't reach their ends.
Inputs may be any that keep to these rules, and one draw needn't show every extreme that they name: `tile_rows`: for every Hamiltonian slot, padded ones too, the block row I does not exceed the block column J. `tile_count`: some device has all 32 slots live in every draw; the live slots of one device name distinct pairs of block row and block column. `dipole_count`: some device has all 32 slots live in every draw.
All inputs are finite; a program needn't handle non-finite values.
Results may differ from the reference program's by a relative error of at most 0.0003.
Values may be sent and summed in bfloat16 or wider, within the bound.
No kernel may reach another device: no remote copies, remote signals or barrier semaphores. Data moves between devices by JAX's collectives and lax.ppermute only.
A program may use at most 128 MiB of HBM per device.

```python
import jax
import jax.numpy as jnp
from jax import lax

NV = 16
SHIFTS = 4
BLOCK = 256
KT = 32
KD = 32
ITERS = 3
ROW_BLOCKS = 8
COL_BLOCKS = 16
STATES = 32768


def tile_layout(key):
    devices = ROW_BLOCKS * COL_BLOCKS
    pairs = ROW_BLOCKS * COL_BLOCKS
    key = jax.random.fold_in(key, 11)
    key_score, key_count, key_full = jax.random.split(key, 3)
    device = jnp.arange(devices, dtype=jnp.int32)[:, None]
    pair = jnp.arange(pairs, dtype=jnp.int32)[None, :]
    upper = device // ROW_BLOCKS * ROW_BLOCKS + pair // COL_BLOCKS
    lower = pair % COL_BLOCKS * ROW_BLOCKS + device % ROW_BLOCKS
    valid = upper <= lower
    score = jax.random.randint(key_score, (devices, pairs), 0, 1 << 20, dtype=jnp.int32) * pairs + pair
    score = jnp.where(valid, score, -1 - pair)
    order = jnp.argsort(-score, axis=1, stable=True).astype(jnp.int32)
    usable = jnp.sum(valid.astype(jnp.int32), axis=1)
    slots = jnp.arange(KT, dtype=jnp.int32)[None, :] % usable[:, None]
    picked = jnp.take_along_axis(order, slots, axis=1)
    count = jax.random.randint(key_count, (devices,), max(1, KT // 4), KT + 1, dtype=jnp.int32)
    count = jnp.maximum(jnp.minimum(count, usable), 1)
    index = jnp.arange(devices, dtype=jnp.int32)
    full_score = jax.random.randint(key_full, (devices,), 0, 1 << 20, dtype=jnp.int32) * devices + index
    full_score = jnp.where(usable >= KT, full_score, -1 - index)
    full = jnp.argsort(-full_score, stable=True)[0].astype(jnp.int32)
    count = jnp.where(index == full, KT, count)
    return ((picked // COL_BLOCKS).reshape(-1), (picked % COL_BLOCKS).reshape(-1), count.astype(jnp.int32))


def dipole_layout(key):
    devices = ROW_BLOCKS * COL_BLOCKS
    key = jax.random.fold_in(key, 23)
    key_rows, key_columns, key_count, key_full = jax.random.split(key, 4)
    rows = jax.random.randint(key_rows, (devices * KD,), 0, ROW_BLOCKS, dtype=jnp.int32)
    columns = jax.random.randint(key_columns, (devices * KD,), 0, COL_BLOCKS, dtype=jnp.int32)
    count = jax.random.randint(key_count, (devices,), max(1, KD // 4), KD + 1, dtype=jnp.int32)
    full = jax.random.randint(key_full, (), 0, devices, dtype=jnp.int32)
    count = jnp.where(jnp.arange(devices, dtype=jnp.int32) == full, KD, count)
    return (rows, columns, count)


def draw_tile_rows(key, part):
    return tile_layout(key)[0]


def draw_tile_columns(key, part):
    return tile_layout(key)[1]


def draw_tile_count(key, part):
    return tile_layout(key)[2]


def draw_dipole_rows(key, part):
    return dipole_layout(key)[0]


def draw_dipole_columns(key, part):
    return dipole_layout(key)[1]


def draw_dipole_count(key, part):
    return dipole_layout(key)[2]


def levels(own_key, extent, cuts, low, largest):
    gain, own = 1.0, jax.random.fold_in(own_key, 6)
    for position, blocks in cuts:
        steps = jnp.exp(jax.random.uniform(jax.random.fold_in(own, position), (blocks,), jnp.float32, low / len(cuts), largest / len(cuts)))
        gain = gain * jnp.repeat(steps, extent[position] // blocks).reshape([-1 if axis == position else 1 for axis in range(len(extent))])
    return gain


def scatter_about(own_key, dims, scale, reach, cuts=(), kind=jnp.bfloat16):
    factor_of = levels(own_key, dims, cuts, -0.22, 0.18) if cuts else 1.0
    drawn = jax.random.normal(own_key, dims, jnp.float32) * scale * factor_of
    return jnp.minimum(jnp.maximum(drawn, -reach), reach).astype(kind)


def setup_inputs(seed: int = 0) -> dict:
    keys = jax.random.split(jax.random.key(seed), 11)
    sources = scatter_about(keys[0], (NV, STATES), 1.0, 6.0, ((1, 128),))
    dipole_tiles = scatter_about(keys[1], (ROW_BLOCKS * COL_BLOCKS * KD, BLOCK, BLOCK), (BLOCK * KD // 8) ** -0.5, 0.1875, ((0, 128),))
    dipole_rows = draw_dipole_rows(jax.random.fold_in(keys[10], 71), 0)
    dipole_columns = draw_dipole_columns(jax.random.fold_in(keys[10], 71), 0)
    dipole_count = draw_dipole_count(jax.random.fold_in(keys[10], 71), 0)
    energies = jnp.clip(jax.random.uniform(keys[5], (STATES,), jnp.float32, -3.0, 3.0) * levels(keys[5], (STATES,), ((0, 128),), -0.4, 0.0), -3.0, 3.0)
    h_tiles = scatter_about(keys[6], (ROW_BLOCKS * COL_BLOCKS * KT, BLOCK, BLOCK), (BLOCK * KT) ** -0.5, 0.0625, ((0, 128),))
    tile_rows = draw_tile_rows(jax.random.fold_in(keys[10], 71), 0)
    tile_columns = draw_tile_columns(jax.random.fold_in(keys[10], 71), 0)
    tile_count = draw_tile_count(jax.random.fold_in(keys[10], 71), 0)
    return dict(sources=sources, dipole_tiles=dipole_tiles, dipole_rows=dipole_rows, dipole_columns=dipole_columns, dipole_count=dipole_count, energies=energies, h_tiles=h_tiles, tile_rows=tile_rows, tile_columns=tile_columns, tile_count=tile_count)


EPSILON = 1e-06

def split_value(vectors):
    upper = vectors.astype(jnp.bfloat16)
    rest = vectors - lax.optimization_barrier(upper).astype(jnp.float32)
    lower = rest.astype(jnp.bfloat16)
    return upper.astype(jnp.float32) + lax.optimization_barrier(lower).astype(jnp.float32)

def block_apply(vectors, tiles, tile_rows, tile_columns, counts, slots, transposed):
    total_blocks = ROW_BLOCKS * COL_BLOCKS
    height = vectors.shape[0]
    blocks = vectors.reshape(height, total_blocks, BLOCK).transpose(1, 0, 2)
    tiles_dev = tiles.reshape(total_blocks, slots, BLOCK, BLOCK)

    def visit(totals, item):
        device, tile_set, row_set, column_set, live_count = item
        upper_block = device // ROW_BLOCKS * ROW_BLOCKS + row_set
        lower_block = column_set * ROW_BLOCKS + device % ROW_BLOCKS
        live = (jnp.arange(slots, dtype=jnp.int32) < live_count).astype(jnp.float32)
        weights = tile_set.astype(jnp.float32)
        picked = blocks[lower_block]
        direct = jnp.einsum('tvs,tks->tvk', picked, weights, precision=lax.Precision.HIGHEST)
        totals = totals.at[upper_block].add(direct * live[:, None, None])
        if transposed:
            picked = blocks[upper_block]
            back = jnp.einsum('tvk,tks->tvs', picked, weights, precision=lax.Precision.HIGHEST)
            totals = totals.at[lower_block].add(back * live[:, None, None])
        return (totals, None)
    start = jnp.zeros((total_blocks, height, BLOCK), jnp.float32)
    totals, unused = lax.scan(visit, start, (jnp.arange(total_blocks, dtype=jnp.int32), tiles_dev, tile_rows.reshape(total_blocks, slots), tile_columns.reshape(total_blocks, slots), counts))
    return totals.transpose(1, 0, 2).reshape(height, total_blocks * BLOCK)

def reference(sources, dipole_tiles, dipole_rows, dipole_columns, dipole_count, energies, h_tiles, tile_rows, tile_columns, tile_count):
    phi = block_apply(sources.astype(jnp.float32), dipole_tiles, dipole_rows, dipole_columns, dipole_count, KD, False)
    rhs = jnp.tile(phi, (SHIFTS, 1))
    centre = (jnp.arange(SHIFTS * NV, dtype=jnp.int32) // NV).astype(jnp.float32)
    shift = (-2.0 + 4.0 * (centre + 0.5) / SHIFTS)[:, None]

    def hamiltonian(vectors):
        return energies[None, :] * vectors + block_apply(split_value(vectors), h_tiles, tile_rows, tile_columns, tile_count, KT, True)

    def lorentz(vectors):
        inner = hamiltonian(vectors) - shift * vectors
        return hamiltonian(inner) - shift * inner + vectors
    solution = jnp.zeros_like(rhs)
    residual = rhs
    direction = rhs
    norm_now = lax.optimization_barrier(jnp.sum(residual * residual, axis=1))
    checks = []
    for index in range(ITERS):
        image = lorentz(direction)
        curvature = lax.optimization_barrier(jnp.sum(direction * image, axis=1))
        image_sum = lax.optimization_barrier(jnp.sum(image, axis=1))
        image_square = lax.optimization_barrier(jnp.sum(image * image, axis=1))
        checks.append(image_sum / jnp.sqrt(image_square + EPSILON))
        alpha = norm_now / curvature
        solution = solution + alpha[:, None] * direction
        residual = residual - alpha[:, None] * image
        norm_next = lax.optimization_barrier(jnp.sum(residual * residual, axis=1))
        direction = residual + (norm_next / norm_now)[:, None] * direction
        norm_now = norm_next
    return (solution, residual, jnp.stack(checks, axis=0))
```

```python
import functools

import jax
import jax.numpy as jnp
from jax import lax
from jax.experimental import pallas as pl
from jax.experimental.pallas import tpu as pltpu
from jax.sharding import PartitionSpec as P

NV = 16
SHIFTS = 4
ITERS = 3
EPSILON = 1e-06
DEGREE = 2 * ITERS
F32 = jnp.float32
BF16 = jnp.bfloat16

VM = pl.BlockSpec(memory_space=pltpu.VMEM)
SM = pl.BlockSpec(memory_space=pltpu.SMEM)


def call(kernel, out_shape, n_smem, n_vmem, scratch=()):
    return pl.pallas_call(
        kernel,
        out_shape=out_shape,
        in_specs=[SM] * n_smem + [VM] * n_vmem,
        out_specs=jax.tree.map(lambda _: VM, out_shape),
        scratch_shapes=list(scratch),
        compiler_params=pltpu.CompilerParams(vmem_limit_bytes=24 << 20),
    )


def split_into(target, index, value):
    upper = value.astype(BF16)
    target[index, :NV] = upper
    target[index, NV:] = (value - upper.astype(F32)).astype(BF16)


def row_sums(a):
    total = a[0]
    for i in range(1, a.shape[0]):
        total = total + a[i]
    return jnp.sum(total, axis=-1, keepdims=True)


def lanes_of(parts, shape):
    lane = lax.broadcasted_iota(jnp.int32, shape, 1)
    out = jnp.zeros(shape, F32)
    for i, part in enumerate(parts):
        out = jnp.where(lane == i, part, out)
    return out


def dots_of(z_mine, z_other, q_mine, q_other, shape):
    norm = row_sums(z_mine * z_mine) + row_sums(z_other * z_other)
    along = row_sums(z_mine * q_mine) + row_sums(z_other * q_other)
    total = row_sums(z_mine) + row_sums(z_other)
    return lanes_of((norm, along, total), shape)


def dipole_kernel(cin, rout, gathered, tiles, p_mine, p_other, xs, acc):
    groups = gathered.shape[0]
    for i in range(groups):
        xs[i] = gathered[i]
    xs[groups] = jnp.zeros(xs.shape[1:], BF16)
    acc[...] = jnp.zeros(acc.shape, F32)
    for t in range(tiles.shape[0]):
        res = lax.dot_general(xs[cin[t]], tiles[t], (((1,), (1,)), ((), ())), preferred_element_type=F32)
        acc[rout[t]] += res
    half = p_mine.shape[0]
    p_mine[...] = acc[:half]
    p_other[...] = acc[half:]


def back_kernel(place, rin, cout, z_mine, z_other, q_mine, q_other, tiles, out, ys):
    half = z_mine.shape[0]
    for i in range(half):
        split_into(ys, i, z_mine[i])
        split_into(ys, half + i, z_other[i])
    ys[2 * half] = jnp.zeros(ys.shape[1:], BF16)
    peers = out.shape[0]
    own = z_mine[place[0]]
    dots = dots_of(z_mine[...], z_other[...], q_mine[...], q_other[...], own.shape)
    for p in range(peers):
        out[p, 0] = own
        out[p, 1] = jnp.zeros_like(own)
        out[p, 2] = dots
    for t in range(tiles.shape[0]):
        res = jnp.dot(ys[rin[t]], tiles[t], preferred_element_type=F32)
        out[cout[t], 1] += res[:NV] + res[NV:]


def direct_kernel(
    has_old, place, cin, rout, gathered, tiles, energies, z_mine, z_other, q_mine, q_other, qp_mine, qp_other, zp_mine, state,
    p_mine, p_other, qn_mine, qn_other, state_out, xs, acc,
):
    groups = gathered.shape[0]
    for i in range(groups):
        split_into(xs, i, gathered[i, 0])
    xs[groups] = jnp.zeros(xs.shape[1:], BF16)
    acc[...] = jnp.zeros(acc.shape, F32)
    for t in range(tiles.shape[0]):
        res = lax.dot_general(xs[cin[t]], tiles[t], (((1,), (1,)), ((), ())), preferred_element_type=F32)
        acc[rout[t]] += res[:NV] + res[NV:]
    back = gathered[0, 1]
    dots = gathered[0, 2]
    for i in range(1, groups):
        back = back + gathered[i, 1]
        dots = dots + gathered[i, 2]
    norm, alpha, total = dots[:, 0:1], dots[:, 1:2], dots[:, 2:3]
    old = state[...]
    s_now, s_old = old[:, 2:3], old[:, 3:4]
    beta = old[:, 1:2] if has_old else jnp.zeros_like(s_now)
    square = norm - alpha * alpha - beta * beta
    beta_next = jnp.sqrt(jnp.maximum(square, 1e-12 * norm + 1e-30))
    scale = 1.0 / beta_next
    s_next = (total - alpha * s_now - beta * s_old) * scale
    state_out[...] = lanes_of((alpha, beta_next, s_next, s_now), state_out.shape)
    qn_mine[...] = (z_mine[...] - alpha * q_mine[...] - beta * qp_mine[...]) * scale
    qn_other[...] = (z_other[...] - alpha * q_other[...] - beta * qp_other[...]) * scale
    own = z_mine[place[0]]
    local = energies[...] * own + back - alpha * own - beta * zp_mine[place[0]]
    acc[place[0]] += local
    half = p_mine.shape[0]
    p_mine[...] = acc[:half] * scale
    p_other[...] = acc[half:] * scale


def apply_h(coefs, alphas, betas, shift):
    out = [None] * (DEGREE + 1)

    def add(j, value):
        out[j] = value if out[j] is None else out[j] + value

    for j, c in enumerate(coefs):
        if c is None:
            continue
        add(j, -shift * c)
        if j + 1 < DEGREE:
            add(j + 1, betas[j + 1] * c)
            add(j, alphas[j] * c)
            if j:
                add(j - 1, betas[j] * c)
        else:
            add(DEGREE, c)
    return out


def vec(op, *vectors):
    return [op(*[0.0 if e is None else e for e in es]) if any(e is not None for e in es) else None for es in zip(*vectors)]


def inner(a, b):
    terms = [x * y for x, y in zip(a, b) if x is not None and y is not None]
    return functools.reduce(lambda x, y: x + y, terms)


def finish_kernel(place, *refs):
    states, qs = refs[:DEGREE], refs[DEGREE : 2 * DEGREE]
    solution_out, partial_out, last_out, aux_out = refs[2 * DEGREE :]
    shape = aux_out.shape[1:]
    lane = lax.broadcasted_iota(jnp.int32, shape, 1)
    shift = -2.0 + 4.0 * (lane.astype(F32) + 0.5) / SHIFTS
    full = [s[...] for s in states]
    spread = lambda a: jnp.broadcast_to(a, shape)
    alphas = [spread(full[j + 1][:, 0:1]) for j in range(DEGREE - 1)]
    betas = [spread(full[j][:, 1:2]) for j in range(DEGREE)]
    sums = [spread(full[j][:, 2:3]) for j in range(DEGREE)]
    residual = [betas[0]] + [None] * DEGREE
    direction = list(residual)
    answer = [None] * (DEGREE + 1)
    norm_now = inner(residual, residual)
    checks = []
    for index in range(ITERS):
        inside = apply_h(direction, alphas, betas, shift)
        image = vec(lambda x, y: x + y, apply_h(inside, alphas, betas, shift), direction)
        curvature = inner(inside, inside) + inner(direction, direction)
        alpha = norm_now / curvature
        if index + 1 < ITERS:
            image_sum = inner(image[:DEGREE], sums)
            checks.append(image_sum / jnp.sqrt(inner(image, image) + EPSILON))
        answer = vec(lambda x, d: x + alpha * d, answer, direction)
        residual = vec(lambda x, d: x - alpha * d, residual, image)
        if index + 1 < ITERS:
            norm_next = inner(residual, residual)
            ratio = norm_next / norm_now
            direction = vec(lambda x, d: x + ratio * d, residual, direction)
            norm_now = norm_next
    known = image[:DEGREE]
    aux_out[0] = checks[0]
    aux_out[1] = checks[1]
    aux_out[2] = inner(known, sums)
    aux_out[3] = inner(known, known)
    aux_out[4] = image[DEGREE]
    aux_out[5] = 2.0 * image[DEGREE] * image[DEGREE - 1]
    aux_out[6] = 2.0 * image[DEGREE] * image[DEGREE - 2] * betas[DEGREE - 1]
    last_out[...] = residual[DEGREE]
    own = [q[place[0]] for q in qs]
    for k in range(SHIFTS):
        rows = slice(k * NV, (k + 1) * NV)
        solution_out[rows] = inner([c[:, k : k + 1] for c in answer[: DEGREE - 1]], own)
        partial_out[rows] = inner([c[:, k : k + 1] for c in residual[:DEGREE]], own)


def tail_kernel(place, z_mine, z_other, q_mine, q_other, partial, last, residual_out, dots_out):
    own = z_mine[place[0]]
    for k in range(SHIFTS):
        rows = slice(k * NV, (k + 1) * NV)
        residual_out[rows] = partial[rows] + last[:, k : k + 1] * own
    dots = dots_of(z_mine[...], z_other[...], q_mine[...], q_other[...], dots_out.shape[1:])
    for p in range(dots_out.shape[0]):
        dots_out[p] = dots


def check_kernel(gathered, aux, out):
    dots = gathered[0]
    for i in range(1, gathered.shape[0]):
        dots = dots + gathered[i]
    norm, along, total = dots[:, 0:1], dots[:, 1:2], dots[:, 2:3]
    image_sum = aux[2] + aux[4] * total
    image_square = aux[3] + aux[4] * aux[4] * norm + aux[5] * along + aux[6]
    rows = (aux[0], aux[1], image_sum / jnp.sqrt(image_square + EPSILON))
    for i, row in enumerate(rows):
        out[i] = jnp.transpose(row)[:SHIFTS]


def body(
    sources,
    dipole_tiles,
    dipole_rows,
    dipole_columns,
    dipole_count,
    energies,
    h_tiles,
    tile_rows,
    tile_columns,
    tile_count,
):
    width = sources.shape[1]
    rows_n = lax.axis_size("row")
    cols_n = lax.axis_size("col")
    half = cols_n // 2
    col = lax.axis_index("col")
    parity = col % 2
    place = (col // 2).reshape(1).astype(jnp.int32)

    def tables(rows, columns, count):
        live = jnp.arange(rows.shape[0], dtype=jnp.int32) < count[0]
        position = ((rows % 2) ^ parity) * half + rows // 2
        return (
            position,
            jnp.where(live, position, cols_n),
            columns,
            jnp.where(live, columns, rows_n),
        )

    d_rout, _, _, d_cin = tables(dipole_rows, dipole_columns, dipole_count)
    h_rout, h_rin, h_cout, h_cin = tables(tile_rows, tile_columns, tile_count)

    pair = [(i, i ^ 1) for i in range(cols_n)]
    ring = lambda d: [(2 * z + k, 2 * ((z + d) % half) + k) for z in range(half) for k in range(2)]

    def group_sum(p_mine, p_other):
        q = p_mine + lax.ppermute(p_other, "col", pair)
        far = lax.ppermute(q, "col", ring(2))
        up = lax.ppermute(q, "col", ring(1))
        down = lax.ppermute(q, "col", ring(3))
        mine = (q + far) + (up + down)
        return mine, lax.ppermute(mine, "col", pair)

    block = jax.ShapeDtypeStruct((half, NV, width), F32)
    small = jax.ShapeDtypeStruct((NV, 128), F32)

    spread = jnp.broadcast_to(sources[None], (rows_n,) + sources.shape)
    gathered = lax.all_to_all(spread, "row", 0, 0, tiled=True)
    p_mine, p_other = call(
        dipole_kernel,
        (block, block),
        2,
        2,
        [pltpu.VMEM((rows_n + 1, NV, width), BF16), pltpu.VMEM((cols_n, NV, width), F32)],
    )(d_cin, d_rout, gathered, dipole_tiles)
    z = group_sum(p_mine, p_other)

    zero = jnp.zeros(block.shape, F32)
    q, q_old, z_old = (zero, zero), (zero, zero), zero
    state = jnp.zeros(small.shape, F32)
    diagonal = energies[None, :]
    states, basis = [], []
    for step in range(DEGREE):
        payload = call(
            back_kernel,
            jax.ShapeDtypeStruct((rows_n, 3, NV, width), F32),
            3,
            5,
            [pltpu.VMEM((cols_n + 1, 2 * NV, width), BF16)],
        )(place, h_rin, h_cout, *z, *q, h_tiles)
        gathered = lax.all_to_all(payload, "row", 0, 0, tiled=True)
        p_mine, p_other, qn_mine, qn_other, state = call(
            functools.partial(direct_kernel, step > 1),
            (block, block, block, block, small),
            3,
            11,
            [pltpu.VMEM((rows_n + 1, 2 * NV, width), BF16), pltpu.VMEM((cols_n, NV, width), F32)],
        )(place, h_cin, h_rout, gathered, h_tiles, diagonal, *z, *q, *q_old, z_old, state)
        states.append(state)
        basis.append(qn_mine)
        z_old = z[0]
        q, q_old = (qn_mine, qn_other), q
        z = group_sum(p_mine, p_other)

    wide = jax.ShapeDtypeStruct((SHIFTS * NV, width), F32)
    answer, partial, last, aux = call(
        finish_kernel,
        (wide, wide, small, jax.ShapeDtypeStruct((7, NV, 128), F32)),
        1,
        2 * DEGREE,
    )(place, *states, *basis)
    residual, dots = call(
        tail_kernel,
        (wide, jax.ShapeDtypeStruct((rows_n, NV, 128), F32)),
        1,
        6,
    )(place, *z, *q, partial, last)
    dots = lax.all_to_all(dots, "row", 0, 0, tiled=True)
    checks = call(check_kernel, jax.ShapeDtypeStruct((ITERS, SHIFTS, NV), F32), 0, 2)(dots, aux)
    return answer, residual, checks.reshape(ITERS, SHIFTS * NV)


def solution(mesh):
    both = ("row", "col")
    return jax.shard_map(
        body,
        mesh=mesh,
        in_specs=(
            P(None, both),
            P(both, None, None),
            P(both),
            P(both),
            P(both),
            P(both),
            P(both, None, None),
            P(both),
            P(both),
            P(both),
        ),
        out_specs=(P(None, both), P(None, both), P()),
        check_vma=False,
    )
```

```python
import functools

import jax
import jax.numpy as jnp
from jax import lax
from jax.experimental import pallas as pl
from jax.experimental.pallas import tpu as pltpu
from jax.sharding import PartitionSpec as P


NV = 16
SHIFTS = 4
ITERS = 3
EPSILON = 1e-06
DEGREE = 2 * ITERS
FLOOR = 0.1
LANES = 128
CHUNKS = 8
F32 = jnp.float32
BF16 = jnp.bfloat16

PLACE_Z, PLACE_ROW, SLOTS = 0, 1, 8
D_FROM, D_TO, DIRECT_FROM, DIRECT_TO, BACK_FROM, BACK_TO = range(6)
ALPHA, BETA, GAMMA, TOTAL, CENTRE, NEXT, GRAM = 0, 1, 2, 3, 4, 5, 8

VM = pl.BlockSpec(memory_space=pltpu.VMEM)
HBM = pl.BlockSpec(memory_space=pltpu.HBM)
SM = pl.BlockSpec(memory_space=pltpu.SMEM)


def call(kernel, out_shape, n_smem, n_vmem, scratch=()):
    return pl.pallas_call(
        kernel,
        out_shape=out_shape,
        in_specs=[SM] * n_smem + [VM] * n_vmem,
        out_specs=jax.tree.map(lambda _: VM, out_shape),
        scratch_shapes=list(scratch),
        compiler_params=pltpu.CompilerParams(vmem_limit_bytes=24 << 20),
    )


def split_into(target, index, value):
    upper = value.astype(BF16)
    target[index, :NV] = upper
    target[index, NV:] = (value - upper.astype(F32)).astype(BF16)


def wide_of(stack, first, parts):
    return jnp.concatenate([stack[first + i * NV : first + (i + 1) * NV] for i in range(parts)], axis=1)


def entry(table, kind, t, slots):
    return table[SLOTS + kind * slots + t]


def row_sum(*blocks):
    total = None
    for a in blocks:
        for i in range(a.shape[0]):
            total = a[i] if total is None else total + a[i]
    return total


def slab_sum(mine, other):
    return jnp.sum(row_sum(mine), axis=-1, keepdims=True) + jnp.sum(row_sum(other), axis=-1, keepdims=True)


def slab_dot(a, b):
    return slab_sum(a[0] * b[0], a[1] * b[1])


def pack(parts):
    lane = lax.broadcasted_iota(jnp.int32, (8, LANES), 1)
    out = jnp.zeros((8, LANES), F32)
    for i, part in enumerate(parts):
        out = jnp.where(lane == i, part[:8], out)
        out = jnp.where(lane == i + LANES // 2, part[8:], out)
    return out


def unpack(dots, i):
    j = i + LANES // 2
    return jnp.concatenate([dots[:, i : i + 1], dots[:, j : j + 1]], axis=0)


def lanes_of(parts, shape):
    lane = lax.broadcasted_iota(jnp.int32, shape, 1)
    out = jnp.zeros(shape, F32)
    for i, part in parts.items():
        out = jnp.where(lane == i, part, out)
    return out


def load_slab(mine, other):
    if len(mine.shape) == 3:
        return mine[...], other[...]
    parts = 2
    half = mine.shape[0] // (parts * NV)
    return tuple(jnp.stack([wide_of(ref, b * parts * NV, parts) for b in range(half)]) for ref in (mine, other))


def dipole_kernel(table, gathered, energies_hbm, tiles_hbm, p_mine, p_other, xs, acc, energies, tiles, sems):
    slots = tiles.shape[0]
    step = slots // CHUNKS
    copies = [
        pltpu.make_async_copy(tiles_hbm.at[pl.ds(c * step, step)], tiles.at[pl.ds(c * step, step)], sems.at[c])
        for c in range(CHUNKS)
    ]
    copies.append(pltpu.make_async_copy(energies_hbm, energies, sems.at[CHUNKS]))
    for copy in copies:
        copy.start()
    groups = gathered.shape[0]
    half = acc.shape[0] // 2
    for i in range(groups):
        xs[i] = gathered[i]
    xs[groups] = jnp.zeros(xs.shape[1:], BF16)
    acc[...] = jnp.zeros(acc.shape, F32)
    for t in range(tiles.shape[0]):
        if t % step == 0:
            copies[t // step].wait()
        x = xs[entry(table, D_FROM, t, slots)]
        res = lax.dot_general(x, tiles[t], (((1,), (1,)), ((), ())), preferred_element_type=F32)
        acc[entry(table, D_TO, t, slots)] += res
    copies[CHUNKS].wait()
    parts = acc.shape[2] // LANES
    for b in range(half):
        for i in range(parts):
            span = slice((b * parts + i) * NV, (b * parts + i + 1) * NV)
            p_mine[span] = acc[b, :, i * LANES : (i + 1) * LANES]
            p_other[span] = acc[half + b, :, i * LANES : (i + 1) * LANES]
    total = jnp.broadcast_to(jnp.sum(energies[...], axis=1, keepdims=True), (8, LANES))
    p_mine[half * parts * NV :] = total
    p_other[half * parts * NV :] = total


def back_kernel(table, z_mine, z_other, *refs):
    tiles, out, ys = refs[-3:]
    qs = [(refs[i], refs[i + 1]) for i in range(0, len(refs) - 3, 2)]
    z = load_slab(z_mine, z_other)
    half = z[0].shape[0]
    slots = tiles.shape[0]
    for i in range(half):
        split_into(ys, i, z[0][i])
        split_into(ys, half + i, z[1][i])
    ys[2 * half] = jnp.zeros(ys.shape[1:], BF16)
    if qs:
        q = [(m[...], o[...]) for m, o in qs]
        dots = [slab_dot(z, z), slab_dot(z, q[-1]), slab_dot(z, q[-2]) if len(q) > 1 else None, slab_sum(*q[-1])]
        dots = [jnp.zeros((NV, 1), F32) if d is None else d for d in dots]
        dots += [slab_dot(q[-1], other) for other in q]
    else:
        centre = z_mine[-8:, 0:1]
        dots = [slab_dot(z, z), jnp.concatenate([centre, centre], axis=0)]
    dots = pack(dots)
    if len(z_mine.shape) == 3:
        own = z_mine[table[PLACE_Z]]
    else:
        own = z[0][0]
        for i in range(1, half):
            own = jnp.where(table[PLACE_Z] == i, z[0][i], own)
    parts = own.shape[1] // LANES
    for p in range(out.shape[0]):
        for i in range(parts):
            out[p, i * NV : (i + 1) * NV] = own[:, i * LANES : (i + 1) * LANES]
            out[p, (parts + i) * NV : (parts + i + 1) * NV] = jnp.zeros((NV, LANES), F32)
        out[p, 2 * parts * NV :] = dots
    for t in range(tiles.shape[0]):
        y = ys[entry(table, BACK_FROM, t, slots)]
        res = jnp.dot(y, tiles[t], preferred_element_type=F32)
        res = res[:NV] + res[NV:]
        peer = entry(table, BACK_TO, t, slots)
        for i in range(parts):
            out[peer, (parts + i) * NV : (parts + i + 1) * NV] += res[:, i * LANES : (i + 1) * LANES]


def direct_kernel(states_n, step, table, gathered, tiles, energies, z_mine, z_other, *refs):
    p_mine, p_other, qn_mine, qn_other, state_out, xs, acc = refs[-7:]
    extra = list(refs[:-7])
    groups = gathered.shape[0]
    half = p_mine.shape[0]
    slots = tiles.shape[0]
    parts = acc.shape[2] // LANES
    for i in range(groups):
        split_into(xs, i, wide_of(gathered[i], 0, parts))
    xs[groups] = jnp.zeros(xs.shape[1:], BF16)
    acc[...] = jnp.zeros(acc.shape, F32)
    for t in range(tiles.shape[0]):
        x = xs[entry(table, DIRECT_FROM, t, slots)]
        res = lax.dot_general(x, tiles[t], (((1,), (1,)), ((), ())), preferred_element_type=F32)
        acc[entry(table, DIRECT_TO, t, slots)] += res[:NV] + res[NV:]
    rest = gathered[0, parts * NV :]
    for i in range(1, groups):
        rest = rest + gathered[i, parts * NV :]
    back = wide_of(rest, 0, parts)
    dots = rest[parts * NV :]
    norm = unpack(dots, 0)
    z = load_slab(z_mine, z_other)
    own = wide_of(gathered[table[PLACE_ROW]], 0, parts)
    lanes = {}
    if step == 0:
        centre = unpack(dots, 1) * (1.0 / states_n)
        beta = jnp.sqrt(norm + 1e-30)
        scale = 1.0 / beta
        qn = [z[0] * scale, z[1] * scale]
        local = (energies[...] - centre) * own + back
    else:
        state = extra[0][...]
        q = (extra[1][...], extra[2][...])
        centre = state[:, CENTRE : CENTRE + 1]
        size = unpack(dots, 3 + step)
        alpha = unpack(dots, 1) / size
        square = norm - alpha * alpha * size
        qn = [z[0] - alpha * q[0], z[1] - alpha * q[1]]
        local = (energies[...] - centre) * own + back - alpha * own
        lanes.update({ALPHA: alpha, TOTAL: unpack(dots, 3)})
        lanes.update({GRAM + i: unpack(dots, 4 + i) for i in range(step)})
        if step > 1:
            old = (extra[3][...], extra[4][...])
            z_old = extra[5]
            size_old = state[:, GRAM + step - 2 : GRAM + step - 1]
            gamma = unpack(dots, 2) / size_old
            square = square - gamma * gamma * size_old
            qn = [a - gamma * b for a, b in zip(qn, old)]
            local = local - gamma * wide_of(z_old[table[PLACE_ROW]], 0, parts)
            lanes[GAMMA] = gamma
        beta_square = jnp.maximum(square, FLOOR * FLOOR * norm) + 1e-30
        beta = jnp.sqrt(beta_square)
        scale = 1.0 / beta
        qn = [a * scale for a in qn]
        lanes[NEXT] = jnp.maximum(square, 0.0) / beta_square
    lanes.update({BETA: beta, CENTRE: centre})
    state_out[...] = lanes_of(lanes, state_out.shape)
    qn_mine[...] = qn[0]
    qn_other[...] = qn[1]
    acc[table[PLACE_Z]] += local
    p_mine[...] = acc[:half] * scale
    p_other[...] = acc[half:] * scale


def apply_h(coefs, alphas, betas, gammas, shift):
    out = [None] * (DEGREE + 1)

    def add(j, value):
        out[j] = value if out[j] is None else out[j] + value

    for j, c in enumerate(coefs):
        if c is None:
            continue
        if j + 1 < DEGREE:
            add(j + 1, betas[j + 1] * c)
            add(j, (alphas[j] - shift) * c)
            if j:
                add(j - 1, gammas[j] * c)
        else:
            add(j, -shift * c)
            add(DEGREE, c)
    return out


def vec(op, *vectors):
    return [op(*[0.0 if e is None else e for e in es]) if any(e is not None for e in es) else None for es in zip(*vectors)]


def total_of(terms):
    return functools.reduce(lambda x, y: x + y, terms)


def finish_kernel(table, *refs):
    states, qs, z_mine = refs[:DEGREE], refs[DEGREE : 2 * DEGREE], refs[2 * DEGREE]
    solution_out, residual_out, aux_out = refs[2 * DEGREE + 1 :]
    shape = aux_out.shape[1:]
    full = [s[...] for s in states]
    spread = lambda step, i: jnp.broadcast_to(full[step][:, i : i + 1], shape)
    lane = lax.broadcasted_iota(jnp.int32, shape, 1)
    shift = -2.0 + 4.0 * (lane.astype(F32) + 0.5) / SHIFTS - spread(0, CENTRE)
    alphas = [spread(j + 1, ALPHA) for j in range(DEGREE - 1)]
    gammas = [None] + [spread(j + 1, GAMMA) for j in range(1, DEGREE - 1)]
    betas = [spread(j, BETA) for j in range(DEGREE)]
    sums = [spread(j + 1, TOTAL) for j in range(DEGREE - 1)]
    gram = [[spread(j + 1, GRAM + i) for i in range(j + 1)] for j in range(DEGREE - 1)]
    gram.append([None] * (DEGREE - 1) + [spread(DEGREE - 1, NEXT)])

    def inner(a, b):
        terms = []
        for j, x in enumerate(a[:DEGREE]):
            for i, y in enumerate(b[:DEGREE]):
                g = gram[max(i, j)][min(i, j)]
                if x is not None and y is not None and g is not None:
                    terms.append(x * (g * y))
        return total_of(terms)

    residual = [betas[0]] + [None] * DEGREE
    direction = list(residual)
    answer = [None] * (DEGREE + 1)
    norm_now = inner(residual, residual)
    for index in range(ITERS):
        inside = apply_h(direction, alphas, betas, gammas, shift)
        image = vec(lambda x, y: x + y, apply_h(inside, alphas, betas, gammas, shift), direction)
        curvature = inner(inside, inside) + inner(direction, direction)
        alpha = norm_now / curvature
        image_sum = total_of([c * s for c, s in zip(image, sums) if c is not None])
        image_square = inner(image, image)
        if index + 1 < ITERS:
            aux_out[index] = image_sum / jnp.sqrt(image_square + EPSILON)
        answer = vec(lambda x, d: x + alpha * d, answer, direction)
        residual = vec(lambda x, d: x - alpha * d, residual, image)
        if index + 1 < ITERS:
            norm_next = inner(residual, residual)
            ratio = norm_next / norm_now
            direction = vec(lambda x, d: x + ratio * d, residual, direction)
            norm_now = norm_next
    aux_out[ITERS - 1] = image_sum
    aux_out[ITERS] = image_square
    for i, c in enumerate(image):
        aux_out[ITERS + 1 + i] = c
    own = [q[table[PLACE_Z]] for q in qs] + [z_mine[table[PLACE_Z]]]
    for k in range(SHIFTS):
        rows = slice(k * NV, (k + 1) * NV)
        solution_out[rows] = total_of([c[:, k : k + 1] * b for c, b in zip(answer, own) if c is not None])
        residual_out[rows] = total_of([c[:, k : k + 1] * b for c, b in zip(residual, own)])


def dots_kernel(*refs):
    arrays, dots_out = [r[...] for r in refs[:-1]], refs[-1]
    z, *q = [(arrays[i], arrays[i + 1]) for i in range(0, len(arrays), 2)]
    dots = pack([slab_dot(z, z), slab_sum(*z), slab_sum(*q[-1])] + [slab_dot(z, b) for b in q])
    for p in range(dots_out.shape[0]):
        dots_out[p] = dots


def check_kernel(gathered, aux, out):
    dots = gathered[0]
    for i in range(1, gathered.shape[0]):
        dots = dots + gathered[i]
    norm, total, total_q = (unpack(dots, i) for i in range(3))
    image = [aux[ITERS + 1 + i] for i in range(DEGREE + 1)]
    last = image[DEGREE]
    image_sum = aux[ITERS - 1] + image[DEGREE - 1] * total_q + last * total
    cross = total_of([image[i] * unpack(dots, 3 + i) for i in range(DEGREE)])
    image_square = aux[ITERS] + last * (2.0 * cross + last * norm)
    checks = [aux[i] for i in range(ITERS - 1)] + [image_sum / jnp.sqrt(image_square + EPSILON)]
    for i, row in enumerate(checks):
        flipped = jnp.transpose(row)
        for k in range(SHIFTS):
            out[i : i + 1, k * NV : (k + 1) * NV] = flipped[k : k + 1]


def body(
    sources,
    dipole_tiles,
    dipole_rows,
    dipole_columns,
    dipole_count,
    energies,
    h_tiles,
    tile_rows,
    tile_columns,
    tile_count,
):
    width = sources.shape[1]
    rows_n = lax.axis_size("row")
    cols_n = lax.axis_size("col")
    half = cols_n // 2
    col = lax.axis_index("col")
    parity = col & 1
    slots = tile_rows.shape[0]

    def slot_lists(rows, columns, count):
        live = jnp.arange(slots, dtype=jnp.int32) < count[0]
        position = ((rows & 1) ^ parity) * half + (rows >> 1)
        return [jnp.where(live, columns, rows_n), position, jnp.where(live, position, cols_n), columns]

    spot = jnp.arange(SLOTS, dtype=jnp.int32)
    spot = jnp.where(spot == PLACE_Z, col >> 1, lax.axis_index("row"))
    table = jnp.concatenate(
        [spot]
        + slot_lists(dipole_rows, dipole_columns, dipole_count)[:2]
        + slot_lists(tile_rows, tile_columns, tile_count)
    ).astype(jnp.int32)

    pair = [(i, i ^ 1) for i in range(cols_n)]
    ring = lambda d: [(2 * z + k, 2 * ((z + d) % half) + k) for z in range(half) for k in range(2)]

    def group_sum(p_mine, p_other):
        q = p_mine + lax.ppermute(p_other, "col", pair)
        moved = []
        for d in (2, 1, 3):
            moved.append(lax.ppermute(q, "col", ring(d)))
        mine = (q + moved[0]) + (moved[1] + moved[2])
        return mine, lax.ppermute(mine, "col", pair)

    block = jax.ShapeDtypeStruct((half, NV, width), F32)
    stack = jax.ShapeDtypeStruct((half * NV * width // LANES + 8, LANES), F32)
    small = jax.ShapeDtypeStruct((NV, LANES), F32)
    diagonal = energies[None]

    spread = jnp.broadcast_to(sources[None], (rows_n,) + sources.shape)
    gathered = lax.all_to_all(spread, "row", 0, 0, tiled=True)
    p_mine, p_other = pl.pallas_call(
        dipole_kernel,
        out_shape=(stack, stack),
        in_specs=[SM, VM, HBM, HBM],
        out_specs=(VM, VM),
        scratch_shapes=[
            pltpu.VMEM((rows_n + 1, NV, width), BF16),
            pltpu.VMEM((cols_n, NV, width), F32),
            pltpu.VMEM(diagonal.shape, F32),
            pltpu.VMEM(dipole_tiles.shape, BF16),
            pltpu.SemaphoreType.DMA((CHUNKS + 1,)),
        ],
        compiler_params=pltpu.CompilerParams(vmem_limit_bytes=24 << 20),
    )(table, gathered, *(pltpu.with_memory_space_constraint(a, pltpu.HBM) for a in (diagonal, dipole_tiles)))
    z = group_sum(p_mine, p_other)

    states, basis, received = [], [], []
    for step in range(DEGREE):
        pairs = [array for q in basis for array in q]
        payload = call(
            back_kernel,
            jax.ShapeDtypeStruct((rows_n, 2 * NV * width // LANES + 8, LANES), F32),
            1,
            3 + len(pairs),
            [pltpu.VMEM((cols_n + 1, 2 * NV, width), BF16)],
        )(table, *z, *pairs, h_tiles)
        received.append(lax.all_to_all(payload, "row", 0, 0, tiled=True))
        extra = []
        if step > 0:
            extra = [states[-1], *basis[-1]]
        if step > 1:
            extra += [*basis[-2], received[-2]]
        p_mine, p_other, qn_mine, qn_other, state = call(
            functools.partial(direct_kernel, float(rows_n * cols_n * width), step),
            (block, block, block, block, small),
            1,
            5 + len(extra),
            [pltpu.VMEM((rows_n + 1, 2 * NV, width), BF16), pltpu.VMEM((cols_n, NV, width), F32)],
        )(table, received[-1], h_tiles, diagonal, *z, *extra)
        states.append(state)
        basis.append((qn_mine, qn_other))
        z = group_sum(p_mine, p_other)

    pairs = [array for q in basis for array in q]
    dots = call(dots_kernel, jax.ShapeDtypeStruct((rows_n, 8, LANES), F32), 0, 2 + len(pairs))(*z, *pairs)
    dots = lax.all_to_all(dots, "row", 0, 0, tiled=True)
    result = jax.ShapeDtypeStruct((SHIFTS * NV, width), F32)
    answer, residual, aux = call(
        finish_kernel,
        (result, result, jax.ShapeDtypeStruct((ITERS + 2 + DEGREE, NV, LANES), F32)),
        1,
        2 * DEGREE + 1,
    )(table, *states, *[q[0] for q in basis], z[0])
    checks = call(check_kernel, jax.ShapeDtypeStruct((ITERS, SHIFTS * NV), F32), 0, 2)(dots, aux)
    return answer, residual, checks


def solution(mesh):
    both = ("row", "col")
    return jax.shard_map(
        body,
        mesh=mesh,
        in_specs=(
            P(None, both),
            P(both, None, None),
            P(both),
            P(both),
            P(both),
            P(both),
            P(both, None, None),
            P(both),
            P(both),
            P(both),
        ),
        out_specs=(P(None, both), P(None, both), P()),
        check_vma=False,
    )
```

```python
import functools

import jax
import jax.numpy as jnp
from jax import lax
from jax.experimental import pallas as pl
from jax.experimental.pallas import tpu as pltpu
from jax.sharding import PartitionSpec as P


NV = 16
SHIFTS = 4
ITERS = 3
EPSILON = 1e-06
DEGREE = 2 * ITERS
FLOOR = 0.1
LANES = 128
CHUNKS = 4
F32 = jnp.float32
BF16 = jnp.bfloat16

PLACE_Z, SLOTS = 0, 8
D_FROM, D_TO, DIRECT_FROM, DIRECT_TO, BACK_FROM, BACK_TO = range(6)
CODE = jnp.int16
TOP = 32767.0
FINE = 16.0
DOTS = 16
LANE_OWN, LANE_BACK = 14, 15
DIGIT, DIGIT_LOW = 16384.0, 32768.0
ALPHA, BETA, GAMMA, TOTAL, CENTRE, NEXT, GRAM = 0, 1, 2, 3, 4, 5, 8

VM = pl.BlockSpec(memory_space=pltpu.VMEM)
HBM = pl.BlockSpec(memory_space=pltpu.HBM)
SM = pl.BlockSpec(memory_space=pltpu.SMEM)


def call(kernel, out_shape, n_smem, n_vmem, scratch=()):
    return pl.pallas_call(
        kernel,
        out_shape=out_shape,
        in_specs=[SM] * n_smem + [VM] * n_vmem,
        out_specs=jax.tree.map(lambda _: VM, out_shape),
        scratch_shapes=list(scratch),
        compiler_params=pltpu.CompilerParams(vmem_limit_bytes=24 << 20),
    )


def split_into(target, index, value):
    upper = value.astype(BF16)
    target[index, :NV] = upper
    target[index, NV:] = (value - upper.astype(F32)).astype(BF16)


def wide_of(stack, first, parts):
    return jnp.concatenate([stack[first + i * NV : first + (i + 1) * NV] for i in range(parts)], axis=1)


def entry(table, kind, t, slots):
    return table[SLOTS + kind * slots + t]


def row_sum(*blocks):
    total = None
    for a in blocks:
        for i in range(a.shape[0]):
            total = a[i] if total is None else total + a[i]
    return total


def slab_sum(mine, other):
    return jnp.sum(row_sum(mine), axis=-1, keepdims=True) + jnp.sum(row_sum(other), axis=-1, keepdims=True)


def slab_dot(a, b):
    return slab_sum(a[0] * b[0], a[1] * b[1])


def pack(parts):
    lane = lax.broadcasted_iota(jnp.int32, (8, LANES), 1)
    out = jnp.zeros((8, LANES), F32)
    for i, part in enumerate(parts):
        out = jnp.where(lane == i, part[:8], out)
        out = jnp.where(lane == i + LANES // 2, part[8:], out)
    return out


def unpack(dots, i):
    j = i + LANES // 2
    return jnp.concatenate([dots[:, i : i + 1], dots[:, j : j + 1]], axis=0)


def lanes_of(parts, shape):
    lane = lax.broadcasted_iota(jnp.int32, shape, 1)
    out = jnp.zeros(shape, F32)
    for i, part in parts.items():
        out = jnp.where(lane == i, part, out)
    return out


def fine_log(block):
    peak = jnp.max(jnp.abs(block), axis=-1, keepdims=True)
    return jnp.ceil(FINE * jnp.log2(jnp.maximum(peak, 1e-30)) + 0.02)


def unit_of(fine):
    return jnp.exp2(fine * (1.0 / FINE)) * (1.0 / TOP)


def code_of(value):
    return jnp.clip(jnp.round(value), -TOP, TOP).astype(jnp.int32).astype(CODE)


def value_of(code):
    return code.astype(jnp.int32).astype(F32)


def encode(parts):
    shape = (NV, LANES)
    numbers = lanes_of(dict(enumerate(parts)), shape)
    power = jnp.ceil(jnp.log2(jnp.maximum(jnp.abs(numbers), 1e-30)))
    digits = numbers * jnp.exp2(-power) * DIGIT
    first = jnp.round(digits)
    second = jnp.round((digits - first) * DIGIT_LOW)
    used = lax.broadcasted_iota(jnp.int32, shape, 1) < DOTS
    power, first, second = (jnp.where(used, a, 0.0) for a in (power, first, second))
    return power + pltpu.roll(first, DOTS, 1) + pltpu.roll(second, 2 * DOTS, 1)


def decode(tile):
    first, second = pltpu.roll(tile, LANES - DOTS, 1), pltpu.roll(tile, LANES - 2 * DOTS, 1)
    return jnp.exp2(tile) * ((first + second * (1.0 / DIGIT_LOW)) * (1.0 / DIGIT))


def own_of(table, z_mine, z):
    if len(z_mine.shape) == 3:
        return z_mine[table[PLACE_Z]]
    own = z[0][0]
    for i in range(1, z[0].shape[0]):
        own = jnp.where(table[PLACE_Z] == i, z[0][i], own)
    return own


def load_slab(mine, other):
    if len(mine.shape) == 3:
        return mine[...], other[...]
    parts = 2
    half = mine.shape[0] // (parts * NV)
    return tuple(jnp.stack([wide_of(ref, b * parts * NV, parts) for b in range(half)]) for ref in (mine, other))


def load_kernel(source, target, sems):
    step = source.shape[0] // CHUNKS
    copies = [
        pltpu.make_async_copy(source.at[pl.ds(c * step, step)], target.at[pl.ds(c * step, step)], sems.at[c])
        for c in range(CHUNKS)
    ]
    for copy in copies:
        copy.start()
    for copy in copies:
        copy.wait()


def dipole_kernel(table, gathered, energies_hbm, tiles_hbm, p_mine, p_other, xs, acc, energies, tiles, sems):
    slots = tiles.shape[0]
    step = slots // CHUNKS
    copies = [
        pltpu.make_async_copy(tiles_hbm.at[pl.ds(c * step, step)], tiles.at[pl.ds(c * step, step)], sems.at[c])
        for c in range(CHUNKS)
    ]
    copies.append(pltpu.make_async_copy(energies_hbm, energies, sems.at[CHUNKS]))
    for copy in copies:
        copy.start()
    groups = gathered.shape[0]
    half = acc.shape[0] // 2
    for i in range(groups):
        xs[i] = gathered[i]
    xs[groups] = jnp.zeros(xs.shape[1:], BF16)
    acc[...] = jnp.zeros(acc.shape, F32)
    for t in range(tiles.shape[0]):
        if t % step == 0:
            copies[t // step].wait()
        x = xs[entry(table, D_FROM, t, slots)]
        res = lax.dot_general(x, tiles[t], (((1,), (1,)), ((), ())), preferred_element_type=F32)
        acc[entry(table, D_TO, t, slots)] += res
    copies[CHUNKS].wait()
    parts = acc.shape[2] // LANES
    for b in range(half):
        for i in range(parts):
            span = slice((b * parts + i) * NV, (b * parts + i + 1) * NV)
            p_mine[span] = acc[b, :, i * LANES : (i + 1) * LANES]
            p_other[span] = acc[half + b, :, i * LANES : (i + 1) * LANES]
    total = jnp.broadcast_to(jnp.sum(energies[...], axis=1, keepdims=True), (8, LANES))
    p_mine[half * parts * NV :] = total
    p_other[half * parts * NV :] = total


def back_kernel(table, z_mine, z_other, *refs):
    tiles, out, ys, acc = refs[-4:]
    qs = [(refs[i], refs[i + 1]) for i in range(0, len(refs) - 4, 2)]
    z = load_slab(z_mine, z_other)
    half = z[0].shape[0]
    slots = tiles.shape[0]
    for i in range(half):
        split_into(ys, i, z[0][i])
        split_into(ys, half + i, z[1][i])
    ys[2 * half] = jnp.zeros(ys.shape[1:], BF16)
    if qs:
        q = [(m[...], o[...]) for m, o in qs]
        dots = [slab_dot(z, z), slab_dot(z, q[-1]), slab_dot(z, q[-2]) if len(q) > 1 else None, slab_sum(*q[-1])]
        dots = [jnp.zeros((NV, 1), F32) if d is None else d for d in dots]
        dots += [slab_dot(q[-1], other) for other in q]
    else:
        centre = z_mine[-8:, 0:1]
        dots = [slab_dot(z, z), jnp.concatenate([centre, centre], axis=0)]
    own = own_of(table, z_mine, z)
    acc[...] = jnp.zeros(acc.shape, F32)
    for t in range(slots):
        y = ys[entry(table, BACK_FROM, t, slots)]
        res = jnp.dot(y, tiles[t], preferred_element_type=F32)
        acc[entry(table, BACK_TO, t, slots)] += res[:NV] + res[NV:]
    parts = own.shape[1] // LANES
    lane = lax.broadcasted_iota(jnp.int32, (NV, LANES), 1)
    fine = fine_log(own)
    own = code_of(own / unit_of(fine))
    numbers = jnp.where(lane == LANE_OWN, fine, encode(dots))
    for p in range(out.shape[0]):
        image = acc[p]
        fine = fine_log(image)
        image = code_of(image / unit_of(fine))
        for i in range(parts):
            out[p, i * NV : (i + 1) * NV] = own[:, i * LANES : (i + 1) * LANES]
            out[p, (parts + i) * NV : (parts + i + 1) * NV] = image[:, i * LANES : (i + 1) * LANES]
        out[p, 2 * parts * NV :] = code_of(jnp.where(lane == LANE_BACK, fine, numbers))


def direct_kernel(states_n, step, table, gathered, tiles, energies, z_mine, z_other, *refs):
    p_mine, p_other, qn_mine, qn_other, state_out, xs, acc = refs[-7:]
    extra = list(refs[:-7])
    groups = gathered.shape[0]
    half = p_mine.shape[0]
    slots = tiles.shape[0]
    parts = acc.shape[2] // LANES
    back = dots = None
    for i in range(groups):
        tile = value_of(gathered[i, 2 * parts * NV :])
        unit = unit_of(tile)
        split_into(xs, i, value_of(wide_of(gathered.at[i], 0, parts)) * unit[:, LANE_OWN : LANE_OWN + 1])
        image = value_of(wide_of(gathered.at[i], parts * NV, parts)) * unit[:, LANE_BACK : LANE_BACK + 1]
        numbers = decode(tile)
        back = image if i == 0 else back + image
        dots = numbers if i == 0 else dots + numbers
    xs[groups] = jnp.zeros(xs.shape[1:], BF16)
    acc[...] = jnp.zeros(acc.shape, F32)
    for t in range(tiles.shape[0]):
        x = xs[entry(table, DIRECT_FROM, t, slots)]
        res = lax.dot_general(x, tiles[t], (((1,), (1,)), ((), ())), preferred_element_type=F32)
        acc[entry(table, DIRECT_TO, t, slots)] += res[:NV] + res[NV:]
    column = lambda i: dots[:, i : i + 1]
    norm = column(0)
    z = load_slab(z_mine, z_other)
    own = own_of(table, z_mine, z)
    lanes = {}
    if step == 0:
        centre = column(1) * (1.0 / states_n)
        beta = jnp.sqrt(norm + 1e-30)
        scale = 1.0 / beta
        qn = [z[0] * scale, z[1] * scale]
        local = (energies[...] - centre) * own + back
    else:
        state = extra[0][...]
        q = (extra[1][...], extra[2][...])
        centre = state[:, CENTRE : CENTRE + 1]
        size = column(3 + step)
        alpha = column(1) / size
        square = norm - alpha * alpha * size
        qn = [z[0] - alpha * q[0], z[1] - alpha * q[1]]
        local = (energies[...] - centre) * own + back - alpha * own
        lanes.update({ALPHA: alpha, TOTAL: column(3)})
        lanes.update({GRAM + i: column(4 + i) for i in range(step)})
        if step > 1:
            old = (extra[3][...], extra[4][...])
            z_old = extra[5]
            size_old = state[:, GRAM + step - 2 : GRAM + step - 1]
            gamma = column(2) / size_old
            square = square - gamma * gamma * size_old
            qn = [a - gamma * b for a, b in zip(qn, old)]
            local = local - gamma * z_old[table[PLACE_Z]]
            lanes[GAMMA] = gamma
        beta_square = jnp.maximum(square, FLOOR * FLOOR * norm) + 1e-30
        beta = jnp.sqrt(beta_square)
        scale = 1.0 / beta
        qn = [a * scale for a in qn]
        lanes[NEXT] = jnp.maximum(square, 0.0) / beta_square
    lanes.update({BETA: beta, CENTRE: centre})
    state_out[...] = lanes_of(lanes, state_out.shape)
    qn_mine[...] = qn[0]
    qn_other[...] = qn[1]
    acc[table[PLACE_Z]] += local
    p_mine[...] = acc[:half] * scale
    p_other[...] = acc[half:] * scale


def apply_h(coefs, alphas, betas, gammas, shift):
    out = [None] * (DEGREE + 1)

    def add(j, value):
        out[j] = value if out[j] is None else out[j] + value

    for j, c in enumerate(coefs):
        if c is None:
            continue
        if j + 1 < DEGREE:
            add(j + 1, betas[j + 1] * c)
            add(j, (alphas[j] - shift) * c)
            if j:
                add(j - 1, gammas[j] * c)
        else:
            add(j, -shift * c)
            add(DEGREE, c)
    return out


def vec(op, *vectors):
    return [op(*[0.0 if e is None else e for e in es]) if any(e is not None for e in es) else None for es in zip(*vectors)]


def total_of(terms):
    return functools.reduce(lambda x, y: x + y, terms)


def finish_kernel(table, *refs):
    states, qs, z_mine = refs[:DEGREE], refs[DEGREE : 2 * DEGREE], refs[2 * DEGREE]
    solution_out, residual_out, aux_out = refs[2 * DEGREE + 1 :]
    shape = aux_out.shape[1:]
    full = [s[...] for s in states]
    spread = lambda step, i: jnp.broadcast_to(full[step][:, i : i + 1], shape)
    lane = lax.broadcasted_iota(jnp.int32, shape, 1)
    shift = -2.0 + 4.0 * (lane.astype(F32) + 0.5) / SHIFTS - spread(0, CENTRE)
    alphas = [spread(j + 1, ALPHA) for j in range(DEGREE - 1)]
    gammas = [None] + [spread(j + 1, GAMMA) for j in range(1, DEGREE - 1)]
    betas = [spread(j, BETA) for j in range(DEGREE)]
    sums = [spread(j + 1, TOTAL) for j in range(DEGREE - 1)]
    gram = [[spread(j + 1, GRAM + i) for i in range(j + 1)] for j in range(DEGREE - 1)]
    gram.append([None] * (DEGREE - 1) + [spread(DEGREE - 1, NEXT)])

    def inner(a, b):
        terms = []
        for j, x in enumerate(a[:DEGREE]):
            for i, y in enumerate(b[:DEGREE]):
                g = gram[max(i, j)][min(i, j)]
                if x is not None and y is not None and g is not None:
                    terms.append(x * (g * y))
        return total_of(terms)

    residual = [betas[0]] + [None] * DEGREE
    direction = list(residual)
    answer = [None] * (DEGREE + 1)
    norm_now = inner(residual, residual)
    for index in range(ITERS):
        inside = apply_h(direction, alphas, betas, gammas, shift)
        image = vec(lambda x, y: x + y, apply_h(inside, alphas, betas, gammas, shift), direction)
        curvature = inner(inside, inside) + inner(direction, direction)
        alpha = norm_now / curvature
        image_sum = total_of([c * s for c, s in zip(image, sums) if c is not None])
        image_square = inner(image, image)
        if index + 1 < ITERS:
            aux_out[index] = image_sum / jnp.sqrt(image_square + EPSILON)
        answer = vec(lambda x, d: x + alpha * d, answer, direction)
        residual = vec(lambda x, d: x - alpha * d, residual, image)
        if index + 1 < ITERS:
            norm_next = inner(residual, residual)
            ratio = norm_next / norm_now
            direction = vec(lambda x, d: x + ratio * d, residual, direction)
            norm_now = norm_next
    aux_out[ITERS - 1] = image_sum
    aux_out[ITERS] = image_square
    for i, c in enumerate(image):
        aux_out[ITERS + 1 + i] = c
    own = [q[table[PLACE_Z]] for q in qs] + [z_mine[table[PLACE_Z]]]
    for k in range(SHIFTS):
        rows = slice(k * NV, (k + 1) * NV)
        solution_out[rows] = total_of([c[:, k : k + 1] * b for c, b in zip(answer, own) if c is not None])
        residual_out[rows] = total_of([c[:, k : k + 1] * b for c, b in zip(residual, own)])


def dots_kernel(*refs):
    arrays, dots_out = [r[...] for r in refs[:-1]], refs[-1]
    z, *q = [(arrays[i], arrays[i + 1]) for i in range(0, len(arrays), 2)]
    dots = pack([slab_dot(z, z), slab_sum(*z), slab_sum(*q[-1])] + [slab_dot(z, b) for b in q])
    for p in range(dots_out.shape[0]):
        dots_out[p] = dots


def check_kernel(gathered, aux, out):
    dots = gathered[0]
    for i in range(1, gathered.shape[0]):
        dots = dots + gathered[i]
    norm, total, total_q = (unpack(dots, i) for i in range(3))
    image = [aux[ITERS + 1 + i] for i in range(DEGREE + 1)]
    last = image[DEGREE]
    image_sum = aux[ITERS - 1] + image[DEGREE - 1] * total_q + last * total
    cross = total_of([image[i] * unpack(dots, 3 + i) for i in range(DEGREE)])
    image_square = aux[ITERS] + last * (2.0 * cross + last * norm)
    checks = [aux[i] for i in range(ITERS - 1)] + [image_sum / jnp.sqrt(image_square + EPSILON)]
    for i, row in enumerate(checks):
        flipped = jnp.transpose(row)
        for k in range(SHIFTS):
            out[i : i + 1, k * NV : (k + 1) * NV] = flipped[k : k + 1]


def body(
    sources,
    dipole_tiles,
    dipole_rows,
    dipole_columns,
    dipole_count,
    energies,
    h_tiles,
    tile_rows,
    tile_columns,
    tile_count,
):
    width = sources.shape[1]
    rows_n = lax.axis_size("row")
    cols_n = lax.axis_size("col")
    half = cols_n // 2
    col = lax.axis_index("col")
    parity = col & 1
    slots = tile_rows.shape[0]

    def slot_lists(rows, columns, count):
        live = jnp.arange(slots, dtype=jnp.int32) < count[0]
        position = ((rows & 1) ^ parity) * half + (rows >> 1)
        return [jnp.where(live, columns, rows_n), position, jnp.where(live, position, cols_n), columns]

    spot = jnp.arange(SLOTS, dtype=jnp.int32)
    spot = jnp.where(spot == PLACE_Z, col >> 1, lax.axis_index("row"))
    table = jnp.concatenate(
        [spot]
        + slot_lists(dipole_rows, dipole_columns, dipole_count)[:2]
        + slot_lists(tile_rows, tile_columns, tile_count)
    ).astype(jnp.int32)

    pair = [(i, i ^ 1) for i in range(cols_n)]
    ring = lambda d: [(2 * z + k, 2 * ((z + (d if k else -d)) % half) + k) for z in range(half) for k in range(2)]

    def group_sum(p_mine, p_other):
        q = p_mine + lax.ppermute(p_other, "col", pair)
        moved = []
        for d in (2, 1, 3):
            moved.append(lax.ppermute(q, "col", ring(d)))
        mine = (q + moved[0]) + (moved[1] + moved[2])
        return mine, lax.ppermute(mine, "col", pair)

    block = jax.ShapeDtypeStruct((half, NV, width), F32)
    stack = jax.ShapeDtypeStruct((half * NV * width // LANES + 8, LANES), F32)
    small = jax.ShapeDtypeStruct((NV, LANES), F32)
    diagonal = energies[None]

    spread = jnp.broadcast_to(sources[None], (rows_n,) + sources.shape)
    gathered = lax.all_to_all(spread, "row", 0, 0, tiled=True)
    p_mine, p_other = pl.pallas_call(
        dipole_kernel,
        out_shape=(stack, stack),
        in_specs=[SM, VM, HBM, HBM],
        out_specs=(VM, VM),
        scratch_shapes=[
            pltpu.VMEM((rows_n + 1, NV, width), BF16),
            pltpu.VMEM((cols_n, NV, width), F32),
            pltpu.VMEM(diagonal.shape, F32),
            pltpu.VMEM(dipole_tiles.shape, BF16),
            pltpu.SemaphoreType.DMA((CHUNKS + 1,)),
        ],
        compiler_params=pltpu.CompilerParams(vmem_limit_bytes=24 << 20),
    )(table, gathered, *(pltpu.with_memory_space_constraint(a, pltpu.HBM) for a in (diagonal, dipole_tiles)))
    p_mine, h_tiles = lax.optimization_barrier((p_mine, pltpu.with_memory_space_constraint(h_tiles, pltpu.HBM)))
    h_tiles = pl.pallas_call(
        load_kernel,
        out_shape=jax.ShapeDtypeStruct(h_tiles.shape, h_tiles.dtype),
        in_specs=[HBM],
        out_specs=VM,
        scratch_shapes=[pltpu.SemaphoreType.DMA((CHUNKS,))],
        compiler_params=pltpu.CompilerParams(vmem_limit_bytes=24 << 20),
    )(h_tiles)
    z = group_sum(p_mine, p_other)

    states, basis, vectors = [], [], []
    for step in range(DEGREE):
        pairs = [array for q in basis for array in q]
        payload = call(
            back_kernel,
            jax.ShapeDtypeStruct((rows_n, 2 * NV * width // LANES + NV, LANES), CODE),
            1,
            3 + len(pairs),
            [pltpu.VMEM((cols_n + 1, 2 * NV, width), BF16), pltpu.VMEM((rows_n, NV, width), F32)],
        )(table, *z, *pairs, h_tiles)
        vectors.append(z[0])
        gathered = lax.all_to_all(payload, "row", 0, 0, tiled=True)
        extra = []
        if step > 0:
            extra = [states[-1], *basis[-1]]
        if step > 1:
            extra += [*basis[-2], vectors[-2]]
        p_mine, p_other, qn_mine, qn_other, state = call(
            functools.partial(direct_kernel, float(rows_n * cols_n * width), step),
            (block, block, block, block, small),
            1,
            5 + len(extra),
            [pltpu.VMEM((rows_n + 1, 2 * NV, width), BF16), pltpu.VMEM((cols_n, NV, width), F32)],
        )(table, gathered, h_tiles, diagonal, *z, *extra)
        states.append(state)
        basis.append((qn_mine, qn_other))
        z = group_sum(p_mine, p_other)

    pairs = [array for q in basis for array in q]
    dots = call(dots_kernel, jax.ShapeDtypeStruct((rows_n, 8, LANES), F32), 0, 2 + len(pairs))(*z, *pairs)
    dots = lax.all_to_all(dots, "row", 0, 0, tiled=True)
    result = jax.ShapeDtypeStruct((SHIFTS * NV, width), F32)
    answer, residual, aux = call(
        finish_kernel,
        (result, result, jax.ShapeDtypeStruct((ITERS + 2 + DEGREE, NV, LANES), F32)),
        1,
        2 * DEGREE + 1,
    )(table, *states, *[q[0] for q in basis], z[0])
    checks = call(check_kernel, jax.ShapeDtypeStruct((ITERS, SHIFTS * NV), F32), 0, 2)(dots, aux)
    return answer, residual, checks


def solution(mesh):
    both = ("row", "col")
    return jax.shard_map(
        body,
        mesh=mesh,
        in_specs=(
            P(None, both),
            P(both, None, None),
            P(both),
            P(both),
            P(both),
            P(both),
            P(both, None, None),
            P(both),
            P(both),
            P(both),
        ),
        out_specs=(P(None, both), P(None, both), P()),
        check_vma=False,
    )
```

```python
import functools

import jax
import jax.numpy as jnp
from jax import lax
from jax.experimental import pallas as pl
from jax.experimental.pallas import tpu as pltpu
from jax.sharding import PartitionSpec as P


NV = 16
SHIFTS = 4
ITERS = 3
EPSILON = 1e-06
DEGREE = 2 * ITERS
FLOOR = 0.1
LANES = 128
CHUNKS = 4
F32 = jnp.float32
BF16 = jnp.bfloat16

PLACE_Z, SLOTS = 0, 8
D_FROM, D_TO, DIRECT_FROM, DIRECT_TO, BACK_FROM, BACK_TO = range(6)
CODE = jnp.int16
TOP = 32767.0
FINE = 16.0
DOTS = 16
LANE_OWN, LANE_BACK = 14, 15
DIGIT, DIGIT_LOW = 16384.0, 32768.0
ALPHA, BETA, GAMMA, TOTAL, CENTRE, NEXT, GRAM = 0, 1, 2, 3, 4, 5, 8

VM = pl.BlockSpec(memory_space=pltpu.VMEM)
HBM = pl.BlockSpec(memory_space=pltpu.HBM)
SM = pl.BlockSpec(memory_space=pltpu.SMEM)


def call(kernel, out_shape, n_smem, n_vmem, scratch=()):
    return pl.pallas_call(
        kernel,
        out_shape=out_shape,
        in_specs=[SM] * n_smem + [VM] * n_vmem,
        out_specs=jax.tree.map(lambda _: VM, out_shape),
        scratch_shapes=list(scratch),
        compiler_params=pltpu.CompilerParams(vmem_limit_bytes=24 << 20),
    )


def split_into(target, index, value):
    upper = value.astype(BF16)
    target[index, :NV] = upper
    target[index, NV:] = (value - upper.astype(F32)).astype(BF16)


def wide_of(stack, first, parts):
    return jnp.concatenate([stack[first + i * NV : first + (i + 1) * NV] for i in range(parts)], axis=1)


def entry(table, kind, t, slots):
    return table[SLOTS + kind * slots + t]


def row_sum(*blocks):
    total = None
    for a in blocks:
        for i in range(a.shape[0]):
            total = a[i] if total is None else total + a[i]
    return total


def slab_sum(mine, other):
    return jnp.sum(row_sum(mine), axis=-1, keepdims=True) + jnp.sum(row_sum(other), axis=-1, keepdims=True)


def slab_dot(a, b):
    return slab_sum(a[0] * b[0], a[1] * b[1])


def pack(parts):
    lane = lax.broadcasted_iota(jnp.int32, (8, LANES), 1)
    out = jnp.zeros((8, LANES), F32)
    for i, part in enumerate(parts):
        out = jnp.where(lane == i, part[:8], out)
        out = jnp.where(lane == i + LANES // 2, part[8:], out)
    return out


def unpack(dots, i):
    j = i + LANES // 2
    return jnp.concatenate([dots[:, i : i + 1], dots[:, j : j + 1]], axis=0)


def lanes_of(parts, shape):
    lane = lax.broadcasted_iota(jnp.int32, shape, 1)
    out = jnp.zeros(shape, F32)
    for i, part in parts.items():
        out = jnp.where(lane == i, part, out)
    return out


def fine_log(block):
    peak = jnp.max(jnp.abs(block), axis=-1, keepdims=True)
    return jnp.ceil(FINE * jnp.log2(jnp.maximum(peak, 1e-30)) + 0.02)


def unit_of(fine):
    return jnp.exp2(fine * (1.0 / FINE)) * (1.0 / TOP)


def code_of(value):
    return jnp.clip(jnp.round(value), -TOP, TOP).astype(jnp.int32).astype(CODE)


def value_of(code):
    return code.astype(jnp.int32).astype(F32)


def put(tile, i, value):
    lane = lax.broadcasted_iota(jnp.int32, tile.shape, 1)
    tile = jnp.where(lane == i, value[:8], tile)
    return jnp.where(lane == i + LANES // 2, value[8:], tile)


def encode(parts):
    numbers = pack(parts)
    power = jnp.ceil(jnp.log2(jnp.maximum(jnp.abs(numbers), 1e-30)))
    digits = numbers * jnp.exp2(-power) * DIGIT
    first = jnp.round(digits)
    second = jnp.round((digits - first) * DIGIT_LOW)
    used = (lax.broadcasted_iota(jnp.int32, numbers.shape, 1) & (LANES // 2 - 1)) < DOTS
    power, first, second = (jnp.where(used, a, 0.0) for a in (power, first, second))
    return power + pltpu.roll(first, DOTS, 1) + pltpu.roll(second, 2 * DOTS, 1)


def decode(tile):
    first, second = pltpu.roll(tile, LANES - DOTS, 1), pltpu.roll(tile, LANES - 2 * DOTS, 1)
    return jnp.exp2(tile) * ((first + second * (1.0 / DIGIT_LOW)) * (1.0 / DIGIT))


def own_of(table, z_mine, z):
    if len(z_mine.shape) == 3:
        return z_mine[table[PLACE_Z]]
    own = z[0][0]
    for i in range(1, z[0].shape[0]):
        own = jnp.where(table[PLACE_Z] == i, z[0][i], own)
    return own


def load_slab(mine, other):
    if len(mine.shape) == 3:
        return mine[...], other[...]
    parts = 2
    half = mine.shape[0] // (parts * NV)
    return tuple(jnp.stack([wide_of(ref, b * parts * NV, parts) for b in range(half)]) for ref in (mine, other))


def load_kernel(source, target, sems):
    step = source.shape[0] // CHUNKS
    copies = [
        pltpu.make_async_copy(source.at[pl.ds(c * step, step)], target.at[pl.ds(c * step, step)], sems.at[c])
        for c in range(CHUNKS)
    ]
    for copy in copies:
        copy.start()
    for copy in copies:
        copy.wait()


def dipole_kernel(table, gathered, energies_hbm, tiles_hbm, p_mine, p_other, xs, acc, energies, tiles, sems):
    slots = tiles.shape[0]
    step = slots // CHUNKS
    copies = [
        pltpu.make_async_copy(tiles_hbm.at[pl.ds(c * step, step)], tiles.at[pl.ds(c * step, step)], sems.at[c])
        for c in range(CHUNKS)
    ]
    copies.append(pltpu.make_async_copy(energies_hbm, energies, sems.at[CHUNKS]))
    for copy in copies:
        copy.start()
    groups = gathered.shape[0]
    half = acc.shape[0] // 2
    for i in range(groups):
        xs[i] = gathered[i]
    xs[groups] = jnp.zeros(xs.shape[1:], BF16)
    acc[...] = jnp.zeros(acc.shape, F32)
    for t in range(tiles.shape[0]):
        if t % step == 0:
            copies[t // step].wait()
        x = xs[entry(table, D_FROM, t, slots)]
        res = lax.dot_general(x, tiles[t], (((1,), (1,)), ((), ())), preferred_element_type=F32)
        acc[entry(table, D_TO, t, slots)] += res
    copies[CHUNKS].wait()
    parts = acc.shape[2] // LANES
    for b in range(half):
        for i in range(parts):
            span = slice((b * parts + i) * NV, (b * parts + i + 1) * NV)
            p_mine[span] = acc[b, :, i * LANES : (i + 1) * LANES]
            p_other[span] = acc[half + b, :, i * LANES : (i + 1) * LANES]
    total = jnp.broadcast_to(jnp.sum(energies[...], axis=1, keepdims=True), (8, LANES))
    p_mine[half * parts * NV :] = total
    p_other[half * parts * NV :] = total


def back_kernel(table, z_mine, z_other, *refs):
    tiles, out, ys, acc = refs[-4:]
    qs = [(refs[i], refs[i + 1]) for i in range(0, len(refs) - 4, 2)]
    z = load_slab(z_mine, z_other)
    half = z[0].shape[0]
    slots = tiles.shape[0]
    for i in range(half):
        split_into(ys, i, z[0][i])
        split_into(ys, half + i, z[1][i])
    ys[2 * half] = jnp.zeros(ys.shape[1:], BF16)
    if qs:
        q = [(m[...], o[...]) for m, o in qs]
        dots = [slab_dot(z, z), slab_dot(z, q[-1]), slab_dot(z, q[-2]) if len(q) > 1 else None, slab_sum(*q[-1])]
        dots = [jnp.zeros((NV, 1), F32) if d is None else d for d in dots]
        dots += [slab_dot(q[-1], other) for other in q]
    else:
        centre = z_mine[-8:, 0:1]
        dots = [slab_dot(z, z), jnp.concatenate([centre, centre], axis=0)]
    own = own_of(table, z_mine, z)
    acc[...] = jnp.zeros(acc.shape, F32)
    for t in range(slots):
        y = ys[entry(table, BACK_FROM, t, slots)]
        res = jnp.dot(y, tiles[t], preferred_element_type=F32)
        acc[entry(table, BACK_TO, t, slots)] += res[:NV] + res[NV:]
    parts = own.shape[1] // LANES
    fine = fine_log(own)
    own = code_of(own / unit_of(fine))
    numbers = put(encode(dots), LANE_OWN, fine)
    for p in range(out.shape[0]):
        image = acc[p]
        fine = fine_log(image)
        image = code_of(image / unit_of(fine))
        for i in range(parts):
            out[p, i * NV : (i + 1) * NV] = own[:, i * LANES : (i + 1) * LANES]
            out[p, (parts + i) * NV : (parts + i + 1) * NV] = image[:, i * LANES : (i + 1) * LANES]
        out[p, 2 * parts * NV :] = code_of(put(numbers, LANE_BACK, fine))


def direct_kernel(states_n, step, table, gathered, tiles, energies, z_mine, z_other, *refs):
    p_mine, p_other, qn_mine, qn_other, state_out, xs, acc = refs[-7:]
    extra = list(refs[:-7])
    groups = gathered.shape[0]
    half = p_mine.shape[0]
    slots = tiles.shape[0]
    parts = acc.shape[2] // LANES
    back = dots = None
    for i in range(groups):
        tile = value_of(gathered[i, 2 * parts * NV :])
        unit = unit_of(tile)
        split_into(xs, i, value_of(wide_of(gathered.at[i], 0, parts)) * unpack(unit, LANE_OWN))
        image = value_of(wide_of(gathered.at[i], parts * NV, parts)) * unpack(unit, LANE_BACK)
        numbers = decode(tile)
        back = image if i == 0 else back + image
        dots = numbers if i == 0 else dots + numbers
    xs[groups] = jnp.zeros(xs.shape[1:], BF16)
    acc[...] = jnp.zeros(acc.shape, F32)
    for t in range(tiles.shape[0]):
        x = xs[entry(table, DIRECT_FROM, t, slots)]
        res = lax.dot_general(x, tiles[t], (((1,), (1,)), ((), ())), preferred_element_type=F32)
        acc[entry(table, DIRECT_TO, t, slots)] += res[:NV] + res[NV:]
    column = functools.partial(unpack, dots)
    norm = column(0)
    z = load_slab(z_mine, z_other)
    own = own_of(table, z_mine, z)
    lanes = {}
    if step == 0:
        centre = column(1) * (1.0 / states_n)
        beta = jnp.sqrt(norm + 1e-30)
        scale = 1.0 / beta
        qn = [z[0] * scale, z[1] * scale]
        local = (energies[...] - centre) * own + back
    else:
        state = extra[0][...]
        q = (extra[1][...], extra[2][...])
        centre = state[:, CENTRE : CENTRE + 1]
        size = column(3 + step)
        alpha = column(1) / size
        square = norm - alpha * alpha * size
        qn = [z[0] - alpha * q[0], z[1] - alpha * q[1]]
        local = (energies[...] - centre) * own + back - alpha * own
        lanes.update({ALPHA: alpha, TOTAL: column(3)})
        lanes.update({GRAM + i: column(4 + i) for i in range(step)})
        if step > 1:
            old = (extra[3][...], extra[4][...])
            z_old = extra[5]
            size_old = state[:, GRAM + step - 2 : GRAM + step - 1]
            gamma = column(2) / size_old
            square = square - gamma * gamma * size_old
            qn = [a - gamma * b for a, b in zip(qn, old)]
            local = local - gamma * z_old[table[PLACE_Z]]
            lanes[GAMMA] = gamma
        beta_square = jnp.maximum(square, FLOOR * FLOOR * norm) + 1e-30
        beta = jnp.sqrt(beta_square)
        scale = 1.0 / beta
        qn = [a * scale for a in qn]
        lanes[NEXT] = jnp.maximum(square, 0.0) / beta_square
    lanes.update({BETA: beta, CENTRE: centre})
    state_out[...] = lanes_of(lanes, state_out.shape)
    qn_mine[...] = qn[0]
    qn_other[...] = qn[1]
    acc[table[PLACE_Z]] += local
    p_mine[...] = acc[:half] * scale
    p_other[...] = acc[half:] * scale


def apply_h(coefs, alphas, betas, gammas, shift):
    out = [None] * (DEGREE + 1)

    def add(j, value):
        out[j] = value if out[j] is None else out[j] + value

    for j, c in enumerate(coefs):
        if c is None:
            continue
        if j + 1 < DEGREE:
            add(j + 1, betas[j + 1] * c)
            add(j, (alphas[j] - shift) * c)
            if j:
                add(j - 1, gammas[j] * c)
        else:
            add(j, -shift * c)
            add(DEGREE, c)
    return out


def vec(op, *vectors):
    return [op(*[0.0 if e is None else e for e in es]) if any(e is not None for e in es) else None for es in zip(*vectors)]


def total_of(terms):
    return functools.reduce(lambda x, y: x + y, terms)


def finish_kernel(table, *refs):
    states, qs, z_mine = refs[:DEGREE], refs[DEGREE : 2 * DEGREE], refs[2 * DEGREE]
    solution_out, residual_out, aux_out = refs[2 * DEGREE + 1 :]
    shape = aux_out.shape[1:]
    full = [s[...] for s in states]
    spread = lambda step, i: jnp.broadcast_to(full[step][:, i : i + 1], shape)
    lane = lax.broadcasted_iota(jnp.int32, shape, 1)
    shift = -2.0 + 4.0 * (lane.astype(F32) + 0.5) / SHIFTS - spread(0, CENTRE)
    alphas = [spread(j + 1, ALPHA) for j in range(DEGREE - 1)]
    gammas = [None] + [spread(j + 1, GAMMA) for j in range(1, DEGREE - 1)]
    betas = [spread(j, BETA) for j in range(DEGREE)]
    sums = [spread(j + 1, TOTAL) for j in range(DEGREE - 1)]
    gram = [[spread(j + 1, GRAM + i) for i in range(j + 1)] for j in range(DEGREE - 1)]
    gram.append([None] * (DEGREE - 1) + [spread(DEGREE - 1, NEXT)])

    def inner(a, b):
        terms = []
        for j, x in enumerate(a[:DEGREE]):
            for i, y in enumerate(b[:DEGREE]):
                g = gram[max(i, j)][min(i, j)]
                if x is not None and y is not None and g is not None:
                    terms.append(x * (g * y))
        return total_of(terms)

    residual = [betas[0]] + [None] * DEGREE
    direction = list(residual)
    answer = [None] * (DEGREE + 1)
    norm_now = inner(residual, residual)
    for index in range(ITERS):
        inside = apply_h(direction, alphas, betas, gammas, shift)
        image = vec(lambda x, y: x + y, apply_h(inside, alphas, betas, gammas, shift), direction)
        curvature = inner(inside, inside) + inner(direction, direction)
        alpha = norm_now / curvature
        image_sum = total_of([c * s for c, s in zip(image, sums) if c is not None])
        image_square = inner(image, image)
        if index + 1 < ITERS:
            aux_out[index] = image_sum / jnp.sqrt(image_square + EPSILON)
        answer = vec(lambda x, d: x + alpha * d, answer, direction)
        residual = vec(lambda x, d: x - alpha * d, residual, image)
        if index + 1 < ITERS:
            norm_next = inner(residual, residual)
            ratio = norm_next / norm_now
            direction = vec(lambda x, d: x + ratio * d, residual, direction)
            norm_now = norm_next
    aux_out[ITERS - 1] = image_sum
    aux_out[ITERS] = image_square
    for i, c in enumerate(image):
        aux_out[ITERS + 1 + i] = c
    own = [q[table[PLACE_Z]] for q in qs] + [z_mine[table[PLACE_Z]]]
    for k in range(SHIFTS):
        rows = slice(k * NV, (k + 1) * NV)
        solution_out[rows] = total_of([c[:, k : k + 1] * b for c, b in zip(answer, own) if c is not None])
        residual_out[rows] = total_of([c[:, k : k + 1] * b for c, b in zip(residual, own)])


def dots_kernel(*refs):
    arrays, dots_out = [r[...] for r in refs[:-1]], refs[-1]
    z, *q = [(arrays[i], arrays[i + 1]) for i in range(0, len(arrays), 2)]
    dots = pack([slab_dot(z, z), slab_sum(*z), slab_sum(*q[-1])] + [slab_dot(z, b) for b in q])
    for p in range(dots_out.shape[0]):
        dots_out[p] = dots


def check_kernel(gathered, aux, out):
    dots = gathered[0]
    for i in range(1, gathered.shape[0]):
        dots = dots + gathered[i]
    norm, total, total_q = (unpack(dots, i) for i in range(3))
    image = [aux[ITERS + 1 + i] for i in range(DEGREE + 1)]
    last = image[DEGREE]
    image_sum = aux[ITERS - 1] + image[DEGREE - 1] * total_q + last * total
    cross = total_of([image[i] * unpack(dots, 3 + i) for i in range(DEGREE)])
    image_square = aux[ITERS] + last * (2.0 * cross + last * norm)
    checks = [aux[i] for i in range(ITERS - 1)] + [image_sum / jnp.sqrt(image_square + EPSILON)]
    for i, row in enumerate(checks):
        flipped = jnp.transpose(row)
        for k in range(SHIFTS):
            out[i : i + 1, k * NV : (k + 1) * NV] = flipped[k : k + 1]


def body(
    sources,
    dipole_tiles,
    dipole_rows,
    dipole_columns,
    dipole_count,
    energies,
    h_tiles,
    tile_rows,
    tile_columns,
    tile_count,
):
    width = sources.shape[1]
    rows_n = lax.axis_size("row")
    cols_n = lax.axis_size("col")
    half = cols_n // 2
    col = lax.axis_index("col")
    parity = col & 1
    slots = tile_rows.shape[0]

    def slot_lists(rows, columns, count):
        live = jnp.arange(slots, dtype=jnp.int32) < count[0]
        position = ((rows & 1) ^ parity) * half + (rows >> 1)
        return [jnp.where(live, columns, rows_n), position, jnp.where(live, position, cols_n), columns]

    spot = jnp.arange(SLOTS, dtype=jnp.int32)
    spot = jnp.where(spot == PLACE_Z, col >> 1, lax.axis_index("row"))
    table = jnp.concatenate(
        [spot]
        + slot_lists(dipole_rows, dipole_columns, dipole_count)[:2]
        + slot_lists(tile_rows, tile_columns, tile_count)
    ).astype(jnp.int32)

    pair = [(i, i ^ 1) for i in range(cols_n)]
    ring = lambda d: [(2 * z + k, 2 * ((z + (d if k else -d)) % half) + k) for z in range(half) for k in range(2)]

    def group_sum(p_mine, p_other):
        q = p_mine + lax.ppermute(p_other, "col", pair)
        moved = []
        for d in (2, 1, 3):
            moved.append(lax.ppermute(q, "col", ring(d)))
        mine = (q + moved[0]) + (moved[1] + moved[2])
        return mine, lax.ppermute(mine, "col", pair)

    block = jax.ShapeDtypeStruct((half, NV, width), F32)
    stack = jax.ShapeDtypeStruct((half * NV * width // LANES + 8, LANES), F32)
    small = jax.ShapeDtypeStruct((NV, LANES), F32)
    diagonal = energies[None]

    spread = jnp.broadcast_to(sources[None], (rows_n,) + sources.shape)
    gathered = lax.all_to_all(spread, "row", 0, 0, tiled=True)
    p_mine, p_other = pl.pallas_call(
        dipole_kernel,
        out_shape=(stack, stack),
        in_specs=[SM, VM, HBM, HBM],
        out_specs=(VM, VM),
        scratch_shapes=[
            pltpu.VMEM((rows_n + 1, NV, width), BF16),
            pltpu.VMEM((cols_n, NV, width), F32),
            pltpu.VMEM(diagonal.shape, F32),
            pltpu.VMEM(dipole_tiles.shape, BF16),
            pltpu.SemaphoreType.DMA((CHUNKS + 1,)),
        ],
        compiler_params=pltpu.CompilerParams(vmem_limit_bytes=24 << 20),
    )(table, gathered, *(pltpu.with_memory_space_constraint(a, pltpu.HBM) for a in (diagonal, dipole_tiles)))
    p_mine, h_tiles = lax.optimization_barrier((p_mine, pltpu.with_memory_space_constraint(h_tiles, pltpu.HBM)))
    h_tiles = pl.pallas_call(
        load_kernel,
        out_shape=jax.ShapeDtypeStruct(h_tiles.shape, h_tiles.dtype),
        in_specs=[HBM],
        out_specs=VM,
        scratch_shapes=[pltpu.SemaphoreType.DMA((CHUNKS,))],
        compiler_params=pltpu.CompilerParams(vmem_limit_bytes=24 << 20),
    )(h_tiles)
    z = group_sum(p_mine, p_other)

    states, basis, vectors = [], [], []
    for step in range(DEGREE):
        pairs = [array for q in basis for array in q]
        payload = call(
            back_kernel,
            jax.ShapeDtypeStruct((rows_n, 2 * NV * width // LANES + 8, LANES), CODE),
            1,
            3 + len(pairs),
            [pltpu.VMEM((cols_n + 1, 2 * NV, width), BF16), pltpu.VMEM((rows_n, NV, width), F32)],
        )(table, *z, *pairs, h_tiles)
        vectors.append(z[0])
        gathered = lax.all_to_all(payload, "row", 0, 0, tiled=True)
        extra = []
        if step > 0:
            extra = [states[-1], *basis[-1]]
        if step > 1:
            extra += [*basis[-2], vectors[-2]]
        p_mine, p_other, qn_mine, qn_other, state = call(
            functools.partial(direct_kernel, float(rows_n * cols_n * width), step),
            (block, block, block, block, small),
            1,
            5 + len(extra),
            [pltpu.VMEM((rows_n + 1, 2 * NV, width), BF16), pltpu.VMEM((cols_n, NV, width), F32)],
        )(table, gathered, h_tiles, diagonal, *z, *extra)
        states.append(state)
        basis.append((qn_mine, qn_other))
        z = group_sum(p_mine, p_other)

    pairs = [array for q in basis for array in q]
    dots = call(dots_kernel, jax.ShapeDtypeStruct((rows_n, 8, LANES), F32), 0, 2 + len(pairs))(*z, *pairs)
    dots = lax.all_to_all(dots, "row", 0, 0, tiled=True)
    result = jax.ShapeDtypeStruct((SHIFTS * NV, width), F32)
    answer, residual, aux = call(
        finish_kernel,
        (result, result, jax.ShapeDtypeStruct((ITERS + 2 + DEGREE, NV, LANES), F32)),
        1,
        2 * DEGREE + 1,
    )(table, *states, *[q[0] for q in basis], z[0])
    checks = call(check_kernel, jax.ShapeDtypeStruct((ITERS, SHIFTS * NV), F32), 0, 2)(dots, aux)
    return answer, residual, checks


def solution(mesh):
    both = ("row", "col")
    return jax.shard_map(
        body,
        mesh=mesh,
        in_specs=(
            P(None, both),
            P(both, None, None),
            P(both),
            P(both),
            P(both),
            P(both),
            P(both, None, None),
            P(both),
            P(both),
            P(both),
        ),
        out_specs=(P(None, both), P(None, both), P()),
        check_vma=False,
    )
```

```python
import functools

import jax
import jax.numpy as jnp
from jax import lax
from jax.experimental import pallas as pl
from jax.experimental.pallas import tpu as pltpu
from jax.sharding import PartitionSpec as P


NV = 16
SHIFTS = 4
ITERS = 3
EPSILON = 1e-06
DEGREE = 2 * ITERS
FLOOR = 0.1
LANES = 128
CHUNKS = 4
F32 = jnp.float32
BF16 = jnp.bfloat16

PLACE_Z, SLOTS = 0, 8
D_FROM, D_TO, DIRECT_FROM, DIRECT_TO, BACK_FROM, BACK_TO = range(6)
CODE = jnp.int16
TOP = 32767.0
FINE = 16.0
DOTS = 16
LANE_OWN, LANE_BACK = 14, 15
DIGIT, DIGIT_LOW = 16384.0, 32768.0
ALPHA, BETA, GAMMA, TOTAL, CENTRE, NEXT, GRAM = 0, 1, 2, 3, 4, 5, 8

VM = pl.BlockSpec(memory_space=pltpu.VMEM)
HBM = pl.BlockSpec(memory_space=pltpu.HBM)
SM = pl.BlockSpec(memory_space=pltpu.SMEM)


def call(kernel, out_shape, n_smem, n_vmem, scratch=()):
    return pl.pallas_call(
        kernel,
        out_shape=out_shape,
        in_specs=[SM] * n_smem + [VM] * n_vmem,
        out_specs=jax.tree.map(lambda _: VM, out_shape),
        scratch_shapes=list(scratch),
        compiler_params=pltpu.CompilerParams(vmem_limit_bytes=24 << 20),
    )


def split_into(target, index, value):
    upper = value.astype(BF16)
    target[index, :NV] = upper
    target[index, NV:] = (value - upper.astype(F32)).astype(BF16)


def wide_of(stack, first, parts):
    return jnp.concatenate([stack[first + i * NV : first + (i + 1) * NV] for i in range(parts)], axis=1)


def entry(table, kind, t, slots):
    return table[SLOTS + kind * slots + t]


def row_sum(*blocks):
    total = None
    for a in blocks:
        for i in range(a.shape[0]):
            total = a[i] if total is None else total + a[i]
    return total


def slab_sum(mine, other):
    return jnp.sum(row_sum(mine), axis=-1, keepdims=True) + jnp.sum(row_sum(other), axis=-1, keepdims=True)


def slab_dot(a, b):
    return slab_sum(a[0] * b[0], a[1] * b[1])


def pack(parts):
    lane = lax.broadcasted_iota(jnp.int32, (8, LANES), 1)
    out = jnp.zeros((8, LANES), F32)
    for i, part in enumerate(parts):
        out = jnp.where(lane == i, part[:8], out)
        out = jnp.where(lane == i + LANES // 2, part[8:], out)
    return out


def unpack(dots, i):
    j = i + LANES // 2
    return jnp.concatenate([dots[:, i : i + 1], dots[:, j : j + 1]], axis=0)


def lanes_of(parts, shape):
    lane = lax.broadcasted_iota(jnp.int32, shape, 1)
    out = jnp.zeros(shape, F32)
    for i, part in parts.items():
        out = jnp.where(lane == i, part, out)
    return out


def fine_log(block):
    peak = jnp.max(jnp.abs(block), axis=-1, keepdims=True)
    return jnp.ceil(FINE * jnp.log2(jnp.maximum(peak, 1e-30)) + 0.02)


def unit_of(fine):
    return jnp.exp2(fine * (1.0 / FINE)) * (1.0 / TOP)


def code_of(value):
    return jnp.clip(jnp.round(value), -TOP, TOP).astype(jnp.int32).astype(CODE)


def value_of(code):
    return code.astype(jnp.int32).astype(F32)


def put(tile, i, value):
    lane = lax.broadcasted_iota(jnp.int32, tile.shape, 1)
    tile = jnp.where(lane == i, value[:8], tile)
    return jnp.where(lane == i + LANES // 2, value[8:], tile)


def encode(parts):
    numbers = pack(parts)
    power = jnp.ceil(jnp.log2(jnp.maximum(jnp.abs(numbers), 1e-30)))
    digits = numbers * jnp.exp2(-power) * DIGIT
    first = jnp.round(digits)
    second = jnp.round((digits - first) * DIGIT_LOW)
    used = (lax.broadcasted_iota(jnp.int32, numbers.shape, 1) & (LANES // 2 - 1)) < DOTS
    power, first, second = (jnp.where(used, a, 0.0) for a in (power, first, second))
    return power + pltpu.roll(first, DOTS, 1) + pltpu.roll(second, 2 * DOTS, 1)


def decode(tile):
    first, second = pltpu.roll(tile, LANES - DOTS, 1), pltpu.roll(tile, LANES - 2 * DOTS, 1)
    return jnp.exp2(tile) * ((first + second * (1.0 / DIGIT_LOW)) * (1.0 / DIGIT))


def own_of(table, z_mine, z):
    if len(z_mine.shape) == 3:
        return z_mine[table[PLACE_Z]]
    own = z[0][0]
    for i in range(1, z[0].shape[0]):
        own = jnp.where(table[PLACE_Z] == i, z[0][i], own)
    return own


def load_slab(mine, other):
    if len(mine.shape) == 3:
        return mine[...], other[...]
    parts = 2
    half = mine.shape[0] // (parts * NV)
    return tuple(jnp.stack([wide_of(ref, b * parts * NV, parts) for b in range(half)]) for ref in (mine, other))


def load_kernel(source, target, flipped, sems):
    step = source.shape[0] // CHUNKS
    copies = [
        pltpu.make_async_copy(source.at[pl.ds(c * step, step)], target.at[pl.ds(c * step, step)], sems.at[c])
        for c in range(CHUNKS)
    ]
    for copy in copies:
        copy.start()
    for c, copy in enumerate(copies):
        copy.wait()
        for t in range(c * step, (c + 1) * step):
            flipped[t] = jnp.transpose(target[t])


def dipole_kernel(table, gathered, energies_hbm, tiles_hbm, p_mine, p_other, xs, acc, energies, tiles, sems):
    slots = tiles.shape[0]
    step = slots // CHUNKS
    copies = [
        pltpu.make_async_copy(tiles_hbm.at[pl.ds(c * step, step)], tiles.at[pl.ds(c * step, step)], sems.at[c])
        for c in range(CHUNKS)
    ]
    copies.append(pltpu.make_async_copy(energies_hbm, energies, sems.at[CHUNKS]))
    for copy in copies:
        copy.start()
    groups = gathered.shape[0]
    half = acc.shape[0] // 2
    for i in range(groups):
        xs[i] = gathered[i]
    xs[groups] = jnp.zeros(xs.shape[1:], BF16)
    acc[...] = jnp.zeros(acc.shape, F32)
    for t in range(tiles.shape[0]):
        if t % step == 0:
            copies[t // step].wait()
        x = xs[entry(table, D_FROM, t, slots)]
        res = lax.dot_general(x, tiles[t], (((1,), (1,)), ((), ())), preferred_element_type=F32)
        acc[entry(table, D_TO, t, slots)] += res
    copies[CHUNKS].wait()
    parts = acc.shape[2] // LANES
    for b in range(half):
        for i in range(parts):
            span = slice((b * parts + i) * NV, (b * parts + i + 1) * NV)
            p_mine[span] = acc[b, :, i * LANES : (i + 1) * LANES]
            p_other[span] = acc[half + b, :, i * LANES : (i + 1) * LANES]
    total = jnp.broadcast_to(jnp.sum(energies[...], axis=1, keepdims=True), (8, LANES))
    p_mine[half * parts * NV :] = total
    p_other[half * parts * NV :] = total


def back_kernel(table, z_mine, z_other, *refs):
    tiles, out, ys, acc = refs[-4:]
    qs = [(refs[i], refs[i + 1]) for i in range(0, len(refs) - 4, 2)]
    z = load_slab(z_mine, z_other)
    half = z[0].shape[0]
    slots = tiles.shape[0]
    for i in range(half):
        split_into(ys, i, z[0][i])
        split_into(ys, half + i, z[1][i])
    ys[2 * half] = jnp.zeros(ys.shape[1:], BF16)
    if qs:
        q = [(m[...], o[...]) for m, o in qs]
        dots = [slab_dot(z, z), slab_dot(z, q[-1]), slab_dot(z, q[-2]) if len(q) > 1 else None, slab_sum(*q[-1])]
        dots = [jnp.zeros((NV, 1), F32) if d is None else d for d in dots]
        dots += [slab_dot(q[-1], other) for other in q]
    else:
        centre = z_mine[-8:, 0:1]
        dots = [slab_dot(z, z), jnp.concatenate([centre, centre], axis=0)]
    own = own_of(table, z_mine, z)
    acc[...] = jnp.zeros(acc.shape, F32)
    for t in range(slots):
        y = ys[entry(table, BACK_FROM, t, slots)]
        res = jnp.dot(y, tiles[t], preferred_element_type=F32)
        acc[entry(table, BACK_TO, t, slots)] += res[:NV] + res[NV:]
    parts = own.shape[1] // LANES
    fine = fine_log(own)
    own = code_of(own / unit_of(fine))
    numbers = put(encode(dots), LANE_OWN, fine)
    for p in range(out.shape[0]):
        image = acc[p]
        fine = fine_log(image)
        image = code_of(image / unit_of(fine))
        for i in range(parts):
            out[p, i * NV : (i + 1) * NV] = own[:, i * LANES : (i + 1) * LANES]
            out[p, (parts + i) * NV : (parts + i + 1) * NV] = image[:, i * LANES : (i + 1) * LANES]
        out[p, 2 * parts * NV :] = code_of(put(numbers, LANE_BACK, fine))


def direct_kernel(states_n, step, table, gathered, tiles, energies, z_mine, z_other, *refs):
    p_mine, p_other, qn_mine, qn_other, state_out, xs, acc = refs[-7:]
    extra = list(refs[:-7])
    groups = gathered.shape[0]
    half = p_mine.shape[0]
    slots = tiles.shape[0]
    parts = acc.shape[2] // LANES
    back = dots = None
    for i in range(groups):
        tile = value_of(gathered[i, 2 * parts * NV :])
        unit = unit_of(tile)
        split_into(xs, i, value_of(wide_of(gathered.at[i], 0, parts)) * unpack(unit, LANE_OWN))
        image = value_of(wide_of(gathered.at[i], parts * NV, parts)) * unpack(unit, LANE_BACK)
        numbers = decode(tile)
        back = image if i == 0 else back + image
        dots = numbers if i == 0 else dots + numbers
    xs[groups] = jnp.zeros(xs.shape[1:], BF16)
    acc[...] = jnp.zeros(acc.shape, F32)
    for t in range(tiles.shape[0]):
        x = xs[entry(table, DIRECT_FROM, t, slots)]
        res = jnp.dot(x, tiles[t], preferred_element_type=F32)
        acc[entry(table, DIRECT_TO, t, slots)] += res[:NV] + res[NV:]
    column = functools.partial(unpack, dots)
    norm = column(0)
    z = load_slab(z_mine, z_other)
    own = own_of(table, z_mine, z)
    lanes = {}
    if step == 0:
        centre = column(1) * (1.0 / states_n)
        beta = jnp.sqrt(norm + 1e-30)
        scale = 1.0 / beta
        qn = [z[0] * scale, z[1] * scale]
        local = (energies[...] - centre) * own + back
    else:
        state = extra[0][...]
        q = (extra[1][...], extra[2][...])
        centre = state[:, CENTRE : CENTRE + 1]
        size = column(3 + step)
        alpha = column(1) / size
        square = norm - alpha * alpha * size
        qn = [z[0] - alpha * q[0], z[1] - alpha * q[1]]
        local = (energies[...] - centre) * own + back - alpha * own
        lanes.update({ALPHA: alpha, TOTAL: column(3)})
        lanes.update({GRAM + i: column(4 + i) for i in range(step)})
        if step > 1:
            old = (extra[3][...], extra[4][...])
            z_old = extra[5]
            size_old = state[:, GRAM + step - 2 : GRAM + step - 1]
            gamma = column(2) / size_old
            square = square - gamma * gamma * size_old
            qn = [a - gamma * b for a, b in zip(qn, old)]
            local = local - gamma * z_old[table[PLACE_Z]]
            lanes[GAMMA] = gamma
        beta_square = jnp.maximum(square, FLOOR * FLOOR * norm) + 1e-30
        beta = jnp.sqrt(beta_square)
        scale = 1.0 / beta
        qn = [a * scale for a in qn]
        lanes[NEXT] = jnp.maximum(square, 0.0) / beta_square
    lanes.update({BETA: beta, CENTRE: centre})
    state_out[...] = lanes_of(lanes, state_out.shape)
    qn_mine[...] = qn[0]
    qn_other[...] = qn[1]
    acc[table[PLACE_Z]] += local
    p_mine[...] = acc[:half] * scale
    p_other[...] = acc[half:] * scale


def apply_h(coefs, alphas, betas, gammas, shift):
    out = [None] * (DEGREE + 1)

    def add(j, value):
        out[j] = value if out[j] is None else out[j] + value

    for j, c in enumerate(coefs):
        if c is None:
            continue
        if j + 1 < DEGREE:
            add(j + 1, betas[j + 1] * c)
            add(j, (alphas[j] - shift) * c)
            if j:
                add(j - 1, gammas[j] * c)
        else:
            add(j, -shift * c)
            add(DEGREE, c)
    return out


def vec(op, *vectors):
    return [op(*[0.0 if e is None else e for e in es]) if any(e is not None for e in es) else None for es in zip(*vectors)]


def total_of(terms):
    return functools.reduce(lambda x, y: x + y, terms)


def finish_kernel(table, *refs):
    states, qs, z_mine = refs[:DEGREE], refs[DEGREE : 2 * DEGREE], refs[2 * DEGREE]
    solution_out, residual_out, aux_out = refs[2 * DEGREE + 1 :]
    shape = aux_out.shape[1:]
    full = [s[...] for s in states]
    spread = lambda step, i: jnp.broadcast_to(full[step][:, i : i + 1], shape)
    lane = lax.broadcasted_iota(jnp.int32, shape, 1)
    shift = -2.0 + 4.0 * (lane.astype(F32) + 0.5) / SHIFTS - spread(0, CENTRE)
    alphas = [spread(j + 1, ALPHA) for j in range(DEGREE - 1)]
    gammas = [None] + [spread(j + 1, GAMMA) for j in range(1, DEGREE - 1)]
    betas = [spread(j, BETA) for j in range(DEGREE)]
    sums = [spread(j + 1, TOTAL) for j in range(DEGREE - 1)]
    gram = [[spread(j + 1, GRAM + i) for i in range(j + 1)] for j in range(DEGREE - 1)]
    gram.append([None] * (DEGREE - 1) + [spread(DEGREE - 1, NEXT)])

    def inner(a, b):
        terms = []
        for j, x in enumerate(a[:DEGREE]):
            for i, y in enumerate(b[:DEGREE]):
                g = gram[max(i, j)][min(i, j)]
                if x is not None and y is not None and g is not None:
                    terms.append(x * (g * y))
        return total_of(terms)

    residual = [betas[0]] + [None] * DEGREE
    direction = list(residual)
    answer = [None] * (DEGREE + 1)
    norm_now = inner(residual, residual)
    for index in range(ITERS):
        inside = apply_h(direction, alphas, betas, gammas, shift)
        image = vec(lambda x, y: x + y, apply_h(inside, alphas, betas, gammas, shift), direction)
        curvature = inner(inside, inside) + inner(direction, direction)
        alpha = norm_now / curvature
        image_sum = total_of([c * s for c, s in zip(image, sums) if c is not None])
        image_square = inner(image, image)
        if index + 1 < ITERS:
            aux_out[index] = image_sum / jnp.sqrt(image_square + EPSILON)
        answer = vec(lambda x, d: x + alpha * d, answer, direction)
        residual = vec(lambda x, d: x - alpha * d, residual, image)
        if index + 1 < ITERS:
            norm_next = inner(residual, residual)
            ratio = norm_next / norm_now
            direction = vec(lambda x, d: x + ratio * d, residual, direction)
            norm_now = norm_next
    aux_out[ITERS - 1] = image_sum
    aux_out[ITERS] = image_square
    for i, c in enumerate(image):
        aux_out[ITERS + 1 + i] = c
    own = [q[table[PLACE_Z]] for q in qs] + [z_mine[table[PLACE_Z]]]
    for k in range(SHIFTS):
        rows = slice(k * NV, (k + 1) * NV)
        solution_out[rows] = total_of([c[:, k : k + 1] * b for c, b in zip(answer, own) if c is not None])
        residual_out[rows] = total_of([c[:, k : k + 1] * b for c, b in zip(residual, own)])


def dots_kernel(*refs):
    arrays, dots_out = [r[...] for r in refs[:-1]], refs[-1]
    z, *q = [(arrays[i], arrays[i + 1]) for i in range(0, len(arrays), 2)]
    dots = pack([slab_dot(z, z), slab_sum(*z), slab_sum(*q[-1])] + [slab_dot(z, b) for b in q])
    for p in range(dots_out.shape[0]):
        dots_out[p] = dots


def check_kernel(gathered, aux, out):
    dots = gathered[0]
    for i in range(1, gathered.shape[0]):
        dots = dots + gathered[i]
    norm, total, total_q = (unpack(dots, i) for i in range(3))
    image = [aux[ITERS + 1 + i] for i in range(DEGREE + 1)]
    last = image[DEGREE]
    image_sum = aux[ITERS - 1] + image[DEGREE - 1] * total_q + last * total
    cross = total_of([image[i] * unpack(dots, 3 + i) for i in range(DEGREE)])
    image_square = aux[ITERS] + last * (2.0 * cross + last * norm)
    checks = [aux[i] for i in range(ITERS - 1)] + [image_sum / jnp.sqrt(image_square + EPSILON)]
    for i, row in enumerate(checks):
        flipped = jnp.transpose(row)
        for k in range(SHIFTS):
            out[i : i + 1, k * NV : (k + 1) * NV] = flipped[k : k + 1]


def body(
    sources,
    dipole_tiles,
    dipole_rows,
    dipole_columns,
    dipole_count,
    energies,
    h_tiles,
    tile_rows,
    tile_columns,
    tile_count,
):
    width = sources.shape[1]
    rows_n = lax.axis_size("row")
    cols_n = lax.axis_size("col")
    half = cols_n // 2
    col = lax.axis_index("col")
    parity = col & 1
    slots = tile_rows.shape[0]

    def slot_lists(rows, columns, count):
        live = jnp.arange(slots, dtype=jnp.int32) < count[0]
        position = ((rows & 1) ^ parity) * half + (rows >> 1)
        return [jnp.where(live, columns, rows_n), position, jnp.where(live, position, cols_n), columns]

    spot = jnp.arange(SLOTS, dtype=jnp.int32)
    spot = jnp.where(spot == PLACE_Z, col >> 1, lax.axis_index("row"))
    table = jnp.concatenate(
        [spot]
        + slot_lists(dipole_rows, dipole_columns, dipole_count)[:2]
        + slot_lists(tile_rows, tile_columns, tile_count)
    ).astype(jnp.int32)

    pair = [(i, i ^ 1) for i in range(cols_n)]
    ring = lambda d: [(2 * z + k, 2 * ((z + (d if k else -d)) % half) + k) for z in range(half) for k in range(2)]

    def group_sum(p_mine, p_other):
        q = p_mine + lax.ppermute(p_other, "col", pair)
        moved = []
        for d in (2, 1, 3):
            moved.append(lax.ppermute(q, "col", ring(d)))
        mine = (q + moved[0]) + (moved[1] + moved[2])
        return mine, lax.ppermute(mine, "col", pair)

    block = jax.ShapeDtypeStruct((half, NV, width), F32)
    stack = jax.ShapeDtypeStruct((half * NV * width // LANES + 8, LANES), F32)
    small = jax.ShapeDtypeStruct((NV, LANES), F32)
    diagonal = energies[None]

    spread = jnp.broadcast_to(sources[None], (rows_n,) + sources.shape)
    gathered = lax.all_to_all(spread, "row", 0, 0, tiled=True)
    p_mine, p_other = pl.pallas_call(
        dipole_kernel,
        out_shape=(stack, stack),
        in_specs=[SM, VM, HBM, HBM],
        out_specs=(VM, VM),
        scratch_shapes=[
            pltpu.VMEM((rows_n + 1, NV, width), BF16),
            pltpu.VMEM((cols_n, NV, width), F32),
            pltpu.VMEM(diagonal.shape, F32),
            pltpu.VMEM(dipole_tiles.shape, BF16),
            pltpu.SemaphoreType.DMA((CHUNKS + 1,)),
        ],
        compiler_params=pltpu.CompilerParams(vmem_limit_bytes=24 << 20),
    )(table, gathered, *(pltpu.with_memory_space_constraint(a, pltpu.HBM) for a in (diagonal, dipole_tiles)))
    p_mine, h_tiles = lax.optimization_barrier((p_mine, pltpu.with_memory_space_constraint(h_tiles, pltpu.HBM)))
    h_tiles, h_flipped = pl.pallas_call(
        load_kernel,
        out_shape=(jax.ShapeDtypeStruct(h_tiles.shape, h_tiles.dtype),) * 2,
        in_specs=[HBM],
        out_specs=(VM, VM),
        scratch_shapes=[pltpu.SemaphoreType.DMA((CHUNKS,))],
        compiler_params=pltpu.CompilerParams(vmem_limit_bytes=24 << 20),
    )(h_tiles)
    z = group_sum(p_mine, p_other)

    states, basis, vectors = [], [], []
    for step in range(DEGREE):
        pairs = [array for q in basis for array in q]
        payload = call(
            back_kernel,
            jax.ShapeDtypeStruct((rows_n, 2 * NV * width // LANES + 8, LANES), CODE),
            1,
            3 + len(pairs),
            [pltpu.VMEM((cols_n + 1, 2 * NV, width), BF16), pltpu.VMEM((rows_n, NV, width), F32)],
        )(table, *z, *pairs, h_tiles)
        vectors.append(z[0])
        gathered = lax.all_to_all(payload, "row", 0, 0, tiled=True)
        extra = []
        if step > 0:
            extra = [states[-1], *basis[-1]]
        if step > 1:
            extra += [*basis[-2], vectors[-2]]
        p_mine, p_other, qn_mine, qn_other, state = call(
            functools.partial(direct_kernel, float(rows_n * cols_n * width), step),
            (block, block, block, block, small),
            1,
            5 + len(extra),
            [pltpu.VMEM((rows_n + 1, 2 * NV, width), BF16), pltpu.VMEM((cols_n, NV, width), F32)],
        )(table, gathered, h_flipped, diagonal, *z, *extra)
        states.append(state)
        basis.append((qn_mine, qn_other))
        z = group_sum(p_mine, p_other)

    pairs = [array for q in basis for array in q]
    dots = call(dots_kernel, jax.ShapeDtypeStruct((rows_n, 8, LANES), F32), 0, 2 + len(pairs))(*z, *pairs)
    dots = lax.all_to_all(dots, "row", 0, 0, tiled=True)
    result = jax.ShapeDtypeStruct((SHIFTS * NV, width), F32)
    answer, residual, aux = call(
        finish_kernel,
        (result, result, jax.ShapeDtypeStruct((ITERS + 2 + DEGREE, NV, LANES), F32)),
        1,
        2 * DEGREE + 1,
    )(table, *states, *[q[0] for q in basis], z[0])
    checks = call(check_kernel, jax.ShapeDtypeStruct((ITERS, SHIFTS * NV), F32), 0, 2)(dots, aux)
    return answer, residual, checks


def solution(mesh):
    both = ("row", "col")
    return jax.shard_map(
        body,
        mesh=mesh,
        in_specs=(
            P(None, both),
            P(both, None, None),
            P(both),
            P(both),
            P(both),
            P(both),
            P(both, None, None),
            P(both),
            P(both),
            P(both),
        ),
        out_specs=(P(None, both), P(None, both), P()),
        check_vma=False,
    )
```

```python
import functools

import jax
import jax.numpy as jnp
from jax import lax
from jax.experimental import pallas as pl
from jax.experimental.pallas import tpu as pltpu
from jax.sharding import PartitionSpec as P


NV = 16
SHIFTS = 4
ITERS = 3
EPSILON = 1e-06
DEGREE = 2 * ITERS
FLOOR = 0.1
LANES = 128
CHUNKS = 4
F32 = jnp.float32
BF16 = jnp.bfloat16

PLACE_Z, SLOTS = 0, 8
D_FROM, D_TO, DIRECT_FROM, DIRECT_TO, BACK_FROM, BACK_TO = range(6)
CODE = jnp.int16
TOP = 32767.0
FINE = 16.0
DOTS = 16
LANE_OWN, LANE_BACK = 14, 15
DIGIT, DIGIT_LOW = 16384.0, 32768.0
ALPHA, BETA, GAMMA, TOTAL, CENTRE, NEXT, GRAM = 0, 1, 2, 3, 4, 5, 8

VM = pl.BlockSpec(memory_space=pltpu.VMEM)
HBM = pl.BlockSpec(memory_space=pltpu.HBM)
SM = pl.BlockSpec(memory_space=pltpu.SMEM)


def call(kernel, out_shape, n_smem, n_vmem, scratch=()):
    return pl.pallas_call(
        kernel,
        out_shape=out_shape,
        in_specs=[SM] * n_smem + [VM] * n_vmem,
        out_specs=jax.tree.map(lambda _: VM, out_shape),
        scratch_shapes=list(scratch),
        compiler_params=pltpu.CompilerParams(vmem_limit_bytes=24 << 20),
    )


def split_into(target, index, value):
    upper = value.astype(BF16)
    target[index, :NV] = upper
    target[index, NV:] = (value - upper.astype(F32)).astype(BF16)


def wide_of(stack, first, parts):
    return jnp.concatenate([stack[first + i * NV : first + (i + 1) * NV] for i in range(parts)], axis=1)


def entry(table, kind, t, slots):
    return table[SLOTS + kind * slots + t]


def row_sum(*blocks):
    total = None
    for a in blocks:
        for i in range(a.shape[0]):
            total = a[i] if total is None else total + a[i]
    return total


def slab_sum(mine, other):
    return jnp.sum(row_sum(mine), axis=-1, keepdims=True) + jnp.sum(row_sum(other), axis=-1, keepdims=True)


def slab_dot(a, b):
    return slab_sum(a[0] * b[0], a[1] * b[1])


def pack(parts):
    lane = lax.broadcasted_iota(jnp.int32, (8, LANES), 1)
    out = jnp.zeros((8, LANES), F32)
    for i, part in enumerate(parts):
        out = jnp.where(lane == i, part[:8], out)
        out = jnp.where(lane == i + LANES // 2, part[8:], out)
    return out


def unpack(dots, i):
    j = i + LANES // 2
    return jnp.concatenate([dots[:, i : i + 1], dots[:, j : j + 1]], axis=0)


def lanes_of(parts, shape):
    lane = lax.broadcasted_iota(jnp.int32, shape, 1)
    out = jnp.zeros(shape, F32)
    for i, part in parts.items():
        out = jnp.where(lane == i, part, out)
    return out


def fine_log(block):
    peak = jnp.max(jnp.abs(block), axis=-1, keepdims=True)
    return jnp.ceil(FINE * jnp.log2(jnp.maximum(peak, 1e-30)) + 0.02)


def unit_of(fine):
    return jnp.exp2(fine * (1.0 / FINE)) * (1.0 / TOP)


def code_of(value):
    return jnp.clip(jnp.round(value), -TOP, TOP).astype(jnp.int32).astype(CODE)


def value_of(code):
    return code.astype(jnp.int32).astype(F32)


def put(tile, i, value):
    lane = lax.broadcasted_iota(jnp.int32, tile.shape, 1)
    tile = jnp.where(lane == i, value[:8], tile)
    return jnp.where(lane == i + LANES // 2, value[8:], tile)


def encode(parts):
    numbers = pack(parts)
    power = jnp.ceil(jnp.log2(jnp.maximum(jnp.abs(numbers), 1e-30)))
    digits = numbers * jnp.exp2(-power) * DIGIT
    first = jnp.round(digits)
    second = jnp.round((digits - first) * DIGIT_LOW)
    used = (lax.broadcasted_iota(jnp.int32, numbers.shape, 1) & (LANES // 2 - 1)) < DOTS
    power, first, second = (jnp.where(used, a, 0.0) for a in (power, first, second))
    return power + pltpu.roll(first, DOTS, 1) + pltpu.roll(second, 2 * DOTS, 1)


def decode(tile):
    first, second = pltpu.roll(tile, LANES - DOTS, 1), pltpu.roll(tile, LANES - 2 * DOTS, 1)
    return jnp.exp2(tile) * ((first + second * (1.0 / DIGIT_LOW)) * (1.0 / DIGIT))


def own_of(table, z_mine, z):
    if len(z_mine.shape) == 3:
        return z_mine[table[PLACE_Z]]
    own = z[0][0]
    for i in range(1, z[0].shape[0]):
        own = jnp.where(table[PLACE_Z] == i, z[0][i], own)
    return own


def load_slab(mine, other):
    if len(mine.shape) == 3:
        return mine[...], other[...]
    parts = 2
    half = mine.shape[0] // (parts * NV)
    return tuple(jnp.stack([wide_of(ref, b * parts * NV, parts) for b in range(half)]) for ref in (mine, other))


def load_kernel(source, target, flipped, sems):
    step = source.shape[0] // CHUNKS
    copies = [
        pltpu.make_async_copy(source.at[pl.ds(c * step, step)], target.at[pl.ds(c * step, step)], sems.at[c])
        for c in range(CHUNKS)
    ]
    for copy in copies:
        copy.start()
    for c, copy in enumerate(copies):
        copy.wait()
        for t in range(c * step, (c + 1) * step):
            flipped[t] = jnp.transpose(target[t])


def dipole_kernel(table, gathered, energies_hbm, tiles_hbm, p_mine, p_other, xs, acc, energies, tiles, sems):
    slots = tiles.shape[0]
    step = slots // CHUNKS
    copies = [
        pltpu.make_async_copy(tiles_hbm.at[pl.ds(c * step, step)], tiles.at[pl.ds(c * step, step)], sems.at[c])
        for c in range(CHUNKS)
    ]
    copies.append(pltpu.make_async_copy(energies_hbm, energies, sems.at[CHUNKS]))
    for copy in copies:
        copy.start()
    groups = gathered.shape[0]
    half = acc.shape[0] // 2
    for i in range(groups):
        xs[i] = gathered[i]
    xs[groups] = jnp.zeros(xs.shape[1:], BF16)
    acc[...] = jnp.zeros(acc.shape, F32)
    for t in range(tiles.shape[0]):
        if t % step == 0:
            copies[t // step].wait()
        x = xs[entry(table, D_FROM, t, slots)]
        res = lax.dot_general(x, tiles[t], (((1,), (1,)), ((), ())), preferred_element_type=F32)
        acc[entry(table, D_TO, t, slots)] += res
    copies[CHUNKS].wait()
    parts = acc.shape[2] // LANES
    for b in range(half):
        for i in range(parts):
            span = slice((b * parts + i) * NV, (b * parts + i + 1) * NV)
            p_mine[span] = acc[b, :, i * LANES : (i + 1) * LANES]
            p_other[span] = acc[half + b, :, i * LANES : (i + 1) * LANES]
    total = jnp.broadcast_to(jnp.sum(energies[...], axis=1, keepdims=True), (8, LANES))
    p_mine[half * parts * NV :] = total
    p_other[half * parts * NV :] = total


def back_kernel(table, z_mine, z_other, *refs):
    tiles, out, ys, acc = refs[-4:]
    qs = [(refs[i], refs[i + 1]) for i in range(0, len(refs) - 4, 2)]
    z = load_slab(z_mine, z_other)
    half = z[0].shape[0]
    slots = tiles.shape[0]
    for i in range(half):
        split_into(ys, i, z[0][i])
        split_into(ys, half + i, z[1][i])
    ys[2 * half] = jnp.zeros(ys.shape[1:], BF16)
    if qs:
        q = [(m[...], o[...]) for m, o in qs]
        dots = [slab_dot(z, z), slab_dot(z, q[-1]), slab_dot(z, q[-2]) if len(q) > 1 else None, slab_sum(*q[-1])]
        dots = [jnp.zeros((NV, 1), F32) if d is None else d for d in dots]
        dots += [slab_dot(q[-1], other) for other in q]
    else:
        centre = z_mine[-8:, 0:1]
        dots = [slab_dot(z, z), jnp.concatenate([centre, centre], axis=0)]
    own = own_of(table, z_mine, z)
    acc[...] = jnp.zeros(acc.shape, F32)
    for t in range(slots):
        y = ys[entry(table, BACK_FROM, t, slots)]
        res = jnp.dot(y, tiles[t], preferred_element_type=F32)
        acc[entry(table, BACK_TO, t, slots)] += res[:NV] + res[NV:]
    parts = own.shape[1] // LANES
    fine = fine_log(own)
    own = code_of(own / unit_of(fine))
    numbers = put(encode(dots), LANE_OWN, fine)
    for p in range(out.shape[0]):
        image = acc[p]
        fine = fine_log(image)
        image = code_of(image / unit_of(fine))
        for i in range(parts):
            out[p, i * NV : (i + 1) * NV] = own[:, i * LANES : (i + 1) * LANES]
            out[p, (parts + i) * NV : (parts + i + 1) * NV] = image[:, i * LANES : (i + 1) * LANES]
        out[p, 2 * parts * NV :] = code_of(put(numbers, LANE_BACK, fine))


def direct_kernel(states_n, step, table, gathered, tiles, energies, z_mine, z_other, *refs):
    p_mine, p_other, state_out, xs, acc = refs[-5:]
    extra = list(refs[:-5])
    groups = gathered.shape[0]
    half = p_mine.shape[0]
    slots = tiles.shape[0]
    parts = acc.shape[2] // LANES
    back = dots = None
    for i in range(groups):
        tile = value_of(gathered[i, 2 * parts * NV :])
        unit = unit_of(tile)
        split_into(xs, i, value_of(wide_of(gathered.at[i], 0, parts)) * unpack(unit, LANE_OWN))
        image = value_of(wide_of(gathered.at[i], parts * NV, parts)) * unpack(unit, LANE_BACK)
        numbers = decode(tile)
        back = image if i == 0 else back + image
        dots = numbers if i == 0 else dots + numbers
    xs[groups] = jnp.zeros(xs.shape[1:], BF16)
    acc[...] = jnp.zeros(acc.shape, F32)
    for t in range(tiles.shape[0]):
        x = xs[entry(table, DIRECT_FROM, t, slots)]
        res = jnp.dot(x, tiles[t], preferred_element_type=F32)
        acc[entry(table, DIRECT_TO, t, slots)] += res[:NV] + res[NV:]
    column = functools.partial(unpack, dots)
    norm = column(0)
    z = load_slab(z_mine, z_other)
    own = own_of(table, z_mine, z)
    lanes = {}
    if step == 0:
        centre = column(1) * (1.0 / states_n)
        beta = jnp.sqrt(norm + 1e-30)
        scale = 1.0 / beta
        local = (energies[...] - centre) * own + back
    else:
        state = extra[0][...]
        centre = state[:, CENTRE : CENTRE + 1]
        size = column(3 + step)
        alpha = column(1) / size
        square = norm - alpha * alpha * size
        local = (energies[...] - centre) * own + back - alpha * own
        lanes.update({ALPHA: alpha, TOTAL: column(3)})
        lanes.update({GRAM + i: column(4 + i) for i in range(step)})
        if step > 1:
            z_old = extra[1]
            size_old = state[:, GRAM + step - 2 : GRAM + step - 1]
            gamma = column(2) / size_old
            square = square - gamma * gamma * size_old
            local = local - gamma * z_old[table[PLACE_Z]]
            lanes[GAMMA] = gamma
        beta_square = jnp.maximum(square, FLOOR * FLOOR * norm) + 1e-30
        beta = jnp.sqrt(beta_square)
        scale = 1.0 / beta
        lanes[NEXT] = jnp.maximum(square, 0.0) / beta_square
    lanes.update({BETA: beta, CENTRE: centre})
    state_out[...] = lanes_of(lanes, state_out.shape)
    acc[table[PLACE_Z]] += local
    p_mine[...] = acc[:half] * scale
    p_other[...] = acc[half:] * scale


def basis_kernel(state, z_mine, z_other, *refs):
    qn = load_slab(z_mine, z_other)
    q, out = refs[:-2], refs[-2:]
    full = state[...]
    for i, lane in enumerate((ALPHA, GAMMA)[: len(q) // 2]):
        qn = [a - full[:, lane : lane + 1] * b[...] for a, b in zip(qn, q[2 * i : 2 * i + 2])]
    scale = 1.0 / full[:, BETA : BETA + 1]
    for target, a in zip(out, qn):
        target[...] = a * scale


def apply_h(coefs, alphas, betas, gammas, shift):
    out = [None] * (DEGREE + 1)

    def add(j, value):
        out[j] = value if out[j] is None else out[j] + value

    for j, c in enumerate(coefs):
        if c is None:
            continue
        if j + 1 < DEGREE:
            add(j + 1, betas[j + 1] * c)
            add(j, (alphas[j] - shift) * c)
            if j:
                add(j - 1, gammas[j] * c)
        else:
            add(j, -shift * c)
            add(DEGREE, c)
    return out


def vec(op, *vectors):
    return [op(*[0.0 if e is None else e for e in es]) if any(e is not None for e in es) else None for es in zip(*vectors)]


def total_of(terms):
    return functools.reduce(lambda x, y: x + y, terms)


def finish_kernel(table, *refs):
    states, qs, z_mine = refs[:DEGREE], refs[DEGREE : 2 * DEGREE], refs[2 * DEGREE]
    solution_out, residual_out, aux_out = refs[2 * DEGREE + 1 :]
    shape = aux_out.shape[1:]
    full = [s[...] for s in states]
    spread = lambda step, i: jnp.broadcast_to(full[step][:, i : i + 1], shape)
    lane = lax.broadcasted_iota(jnp.int32, shape, 1)
    shift = -2.0 + 4.0 * (lane.astype(F32) + 0.5) / SHIFTS - spread(0, CENTRE)
    alphas = [spread(j + 1, ALPHA) for j in range(DEGREE - 1)]
    gammas = [None] + [spread(j + 1, GAMMA) for j in range(1, DEGREE - 1)]
    betas = [spread(j, BETA) for j in range(DEGREE)]
    sums = [spread(j + 1, TOTAL) for j in range(DEGREE - 1)]
    gram = [[spread(j + 1, GRAM + i) for i in range(j + 1)] for j in range(DEGREE - 1)]
    gram.append([None] * (DEGREE - 1) + [spread(DEGREE - 1, NEXT)])

    def inner(a, b):
        terms = []
        for j, x in enumerate(a[:DEGREE]):
            for i, y in enumerate(b[:DEGREE]):
                g = gram[max(i, j)][min(i, j)]
                if x is not None and y is not None and g is not None:
                    terms.append(x * (g * y))
        return total_of(terms)

    residual = [betas[0]] + [None] * DEGREE
    direction = list(residual)
    answer = [None] * (DEGREE + 1)
    norm_now = inner(residual, residual)
    for index in range(ITERS):
        inside = apply_h(direction, alphas, betas, gammas, shift)
        image = vec(lambda x, y: x + y, apply_h(inside, alphas, betas, gammas, shift), direction)
        curvature = inner(inside, inside) + inner(direction, direction)
        alpha = norm_now / curvature
        image_sum = total_of([c * s for c, s in zip(image, sums) if c is not None])
        image_square = inner(image, image)
        if index + 1 < ITERS:
            aux_out[index] = image_sum / jnp.sqrt(image_square + EPSILON)
        answer = vec(lambda x, d: x + alpha * d, answer, direction)
        residual = vec(lambda x, d: x - alpha * d, residual, image)
        if index + 1 < ITERS:
            norm_next = inner(residual, residual)
            ratio = norm_next / norm_now
            direction = vec(lambda x, d: x + ratio * d, residual, direction)
            norm_now = norm_next
    aux_out[ITERS - 1] = image_sum
    aux_out[ITERS] = image_square
    for i, c in enumerate(image):
        aux_out[ITERS + 1 + i] = c
    own = [q[table[PLACE_Z]] for q in qs] + [z_mine[table[PLACE_Z]]]
    for k in range(SHIFTS):
        rows = slice(k * NV, (k + 1) * NV)
        solution_out[rows] = total_of([c[:, k : k + 1] * b for c, b in zip(answer, own) if c is not None])
        residual_out[rows] = total_of([c[:, k : k + 1] * b for c, b in zip(residual, own)])


def dots_kernel(*refs):
    arrays, dots_out = [r[...] for r in refs[:-1]], refs[-1]
    z, *q = [(arrays[i], arrays[i + 1]) for i in range(0, len(arrays), 2)]
    dots = pack([slab_dot(z, z), slab_sum(*z), slab_sum(*q[-1])] + [slab_dot(z, b) for b in q])
    for p in range(dots_out.shape[0]):
        dots_out[p] = dots


def check_kernel(gathered, aux, out):
    dots = gathered[0]
    for i in range(1, gathered.shape[0]):
        dots = dots + gathered[i]
    norm, total, total_q = (unpack(dots, i) for i in range(3))
    image = [aux[ITERS + 1 + i] for i in range(DEGREE + 1)]
    last = image[DEGREE]
    image_sum = aux[ITERS - 1] + image[DEGREE - 1] * total_q + last * total
    cross = total_of([image[i] * unpack(dots, 3 + i) for i in range(DEGREE)])
    image_square = aux[ITERS] + last * (2.0 * cross + last * norm)
    checks = [aux[i] for i in range(ITERS - 1)] + [image_sum / jnp.sqrt(image_square + EPSILON)]
    for i, row in enumerate(checks):
        flipped = jnp.transpose(row)
        for k in range(SHIFTS):
            out[i : i + 1, k * NV : (k + 1) * NV] = flipped[k : k + 1]


def body(
    sources,
    dipole_tiles,
    dipole_rows,
    dipole_columns,
    dipole_count,
    energies,
    h_tiles,
    tile_rows,
    tile_columns,
    tile_count,
):
    width = sources.shape[1]
    rows_n = lax.axis_size("row")
    cols_n = lax.axis_size("col")
    half = cols_n // 2
    col = lax.axis_index("col")
    parity = col & 1
    slots = tile_rows.shape[0]

    def slot_lists(rows, columns, count):
        live = jnp.arange(slots, dtype=jnp.int32) < count[0]
        position = ((rows & 1) ^ parity) * half + (rows >> 1)
        return [jnp.where(live, columns, rows_n), position, jnp.where(live, position, cols_n), columns]

    spot = jnp.arange(SLOTS, dtype=jnp.int32)
    spot = jnp.where(spot == PLACE_Z, col >> 1, lax.axis_index("row"))
    table = jnp.concatenate(
        [spot]
        + slot_lists(dipole_rows, dipole_columns, dipole_count)[:2]
        + slot_lists(tile_rows, tile_columns, tile_count)
    ).astype(jnp.int32)

    pair = [(i, i ^ 1) for i in range(cols_n)]
    ring = lambda d: [(2 * z + k, 2 * ((z + (d if k else -d)) % half) + k) for z in range(half) for k in range(2)]

    def group_sum(p_mine, p_other):
        q = p_mine + lax.ppermute(p_other, "col", pair)
        moved = []
        for d in (2, 1, 3):
            moved.append(lax.ppermute(q, "col", ring(d)))
        mine = (q + moved[0]) + (moved[1] + moved[2])
        return mine, lax.ppermute(mine, "col", pair)

    block = jax.ShapeDtypeStruct((half, NV, width), F32)
    stack = jax.ShapeDtypeStruct((half * NV * width // LANES + 8, LANES), F32)
    small = jax.ShapeDtypeStruct((NV, LANES), F32)
    diagonal = energies[None]

    spread = jnp.broadcast_to(sources[None], (rows_n,) + sources.shape)
    gathered = lax.all_to_all(spread, "row", 0, 0, tiled=True)
    p_mine, p_other = pl.pallas_call(
        dipole_kernel,
        out_shape=(stack, stack),
        in_specs=[SM, VM, HBM, HBM],
        out_specs=(VM, VM),
        scratch_shapes=[
            pltpu.VMEM((rows_n + 1, NV, width), BF16),
            pltpu.VMEM((cols_n, NV, width), F32),
            pltpu.VMEM(diagonal.shape, F32),
            pltpu.VMEM(dipole_tiles.shape, BF16),
            pltpu.SemaphoreType.DMA((CHUNKS + 1,)),
        ],
        compiler_params=pltpu.CompilerParams(vmem_limit_bytes=24 << 20),
    )(table, gathered, *(pltpu.with_memory_space_constraint(a, pltpu.HBM) for a in (diagonal, dipole_tiles)))
    p_mine, h_tiles = lax.optimization_barrier((p_mine, pltpu.with_memory_space_constraint(h_tiles, pltpu.HBM)))
    h_tiles, h_flipped = pl.pallas_call(
        load_kernel,
        out_shape=(jax.ShapeDtypeStruct(h_tiles.shape, h_tiles.dtype),) * 2,
        in_specs=[HBM],
        out_specs=(VM, VM),
        scratch_shapes=[pltpu.SemaphoreType.DMA((CHUNKS,))],
        compiler_params=pltpu.CompilerParams(vmem_limit_bytes=24 << 20),
    )(h_tiles)
    z = group_sum(p_mine, p_other)

    states, basis, vectors = [], [], []
    for step in range(DEGREE):
        pairs = [array for q in basis for array in q]
        payload = call(
            back_kernel,
            jax.ShapeDtypeStruct((rows_n, 2 * NV * width // LANES + 8, LANES), CODE),
            1,
            3 + len(pairs),
            [pltpu.VMEM((cols_n + 1, 2 * NV, width), BF16), pltpu.VMEM((rows_n, NV, width), F32)],
        )(table, *z, *pairs, h_tiles)
        vectors.append(z[0])
        gathered = lax.all_to_all(payload, "row", 0, 0, tiled=True)
        extra = []
        if step > 0:
            extra = [states[-1]]
        if step > 1:
            extra += [vectors[-2]]
        p_mine, p_other, state = call(
            functools.partial(direct_kernel, float(rows_n * cols_n * width), step),
            (block, block, small),
            1,
            5 + len(extra),
            [pltpu.VMEM((rows_n + 1, 2 * NV, width), BF16), pltpu.VMEM((cols_n, NV, width), F32)],
        )(table, gathered, h_flipped, diagonal, *z, *extra)
        states.append(state)
        before = [array for q in basis[:-3:-1] for array in q]
        basis.append(call(basis_kernel, (block, block), 0, 3 + len(before))(state, *z, *before))
        z = group_sum(p_mine, p_other)

    pairs = [array for q in basis for array in q]
    dots = call(dots_kernel, jax.ShapeDtypeStruct((rows_n, 8, LANES), F32), 0, 2 + len(pairs))(*z, *pairs)
    dots = lax.all_to_all(dots, "row", 0, 0, tiled=True)
    result = jax.ShapeDtypeStruct((SHIFTS * NV, width), F32)
    answer, residual, aux = call(
        finish_kernel,
        (result, result, jax.ShapeDtypeStruct((ITERS + 2 + DEGREE, NV, LANES), F32)),
        1,
        2 * DEGREE + 1,
    )(table, *states, *[q[0] for q in basis], z[0])
    checks = call(check_kernel, jax.ShapeDtypeStruct((ITERS, SHIFTS * NV), F32), 0, 2)(dots, aux)
    return answer, residual, checks


def solution(mesh):
    both = ("row", "col")
    return jax.shard_map(
        body,
        mesh=mesh,
        in_specs=(
            P(None, both),
            P(both, None, None),
            P(both),
            P(both),
            P(both),
            P(both),
            P(both, None, None),
            P(both),
            P(both),
            P(both),
        ),
        out_specs=(P(None, both), P(None, both), P()),
        check_vma=False,
    )
```
